32 devices in a mesh: grp: 2 (over x), seq: 4 (over y, core), sub: 4 (over z).
Axes of the slice: x: 2, y: 2, z: 4, core: 2. Of those that a mesh axis runs over, the one named last changes fastest.
Arguments:
- query_rows: bfloat16 [8, 512, 2048], P(('grp', 'sub'), 'seq'), parts along dimension 0, may hold values from -9 to 9
- key_rows: bfloat16 [8, 512, 256], P(('grp', 'sub'), 'seq'), parts along dimension 0, may hold values from -4 to 4
- value_rows: bfloat16 [8, 512, 256], P(('grp', 'sub'), 'seq'), parts along dimension 0, may hold values from -6 to 6
- residual_in: bfloat16 [8, 512, 2048], P(('grp', 'sub'), 'seq'), parts along dimension 0, may hold values from -6 to 6
- out_proj: bfloat16 [2048, 2048], P('seq'), may hold values from -0.5 to 0.5
- norm_gain: bfloat16 [2048], replicated, may hold values from 0.099609375 to 1.8984375
- expert_ids: int32 [8, 512, 8], P(('grp', 'sub'), 'seq'), parts along dimension 0, may hold values from 0 to 15, all different within a row; in each aligned block of 128 rows (0 to 127, 128 to 255, ..., all dimensions but the last counted through in order) at most 80 rows name the same one
- gate_weights: bfloat16 [8, 512, 8], P(('grp', 'sub'), 'seq'), parts along dimension 0, may hold values from 0.049804688 to 1
- expert_gate: bfloat16 [16, 2048, 768], P(('seq', 'sub')), may hold values from -0.125 to 0.125
- expert_up: bfloat16 [16, 2048, 768], P(('seq', 'sub')), may hold values from -0.125 to 0.125
- expert_down: bfloat16 [16, 768, 2048], P(('seq', 'sub')), may hold values from -0.21875 to 0.21875
Outputs:
- layer_out: bfloat16 [8, 512, 2048], P(('grp', 'sub'), 'seq'), parts along dimension 0
The draws below stay inside these ranges and needn't reach their ends.
There are 2 independent parts, one for each index of `grp`. The reference program is written for one: setup_inputs(seed, part) draws one part's arguments, and reference() takes and returns one part's arrays. A program takes and returns all parts, laid end to end along the dimension named above; an argument that names none is the same for every part. Nothing has to cross between parts.
Inputs may be any that keep to these rules, and one draw needn't show every extreme that they name: `expert_ids`: A row names 8 different experts. In each aligned block of 128 rows (the rows of one device) no expert is named by more than 80 rows, a bound that some block reaches.
All inputs are finite; a program needn't handle non-finite values.
Results may differ from the reference program's by a relative error of at most 0.013.
Values may be sent and summed in bfloat16 or wider, within the bound.
A program may use at most 128 MiB of HBM per device.

```python
import math
import jax
import jax.numpy as jnp
import numpy as np
from jax import lax

D = 2048
HD = 128
QH = 16
KVH = 2
FF = 768
TOPK = 8
TOK_DEV = 128
SEQS = 4
SEQ_LEN = 512
EXPERTS = 16
CAP = 80


def draw_attention(key):
    query_key = jax.random.fold_in(key, 101)
    other_key = jax.random.fold_in(key, 202)
    query_shape = (SEQS, SEQ_LEN, QH * HD)
    key_shape = (SEQS, SEQ_LEN, KVH * HD)
    queries = 2.0 * jax.random.truncated_normal(query_key, -4.0, 4.0, query_shape, jnp.float32)
    keys = jax.random.truncated_normal(other_key, -4.0, 4.0, key_shape, jnp.float32)
    return (queries, keys)


def draw_query_rows(key, part):
    return draw_attention(key)[0].astype(jnp.bfloat16)


def draw_key_rows(key, part):
    return draw_attention(key)[1].astype(jnp.bfloat16)


def steps_of(rng, shape, split, least, largest):
    loudness, own = 1.0, jax.random.fold_in(rng, 6)
    for axis_at, parts in split:
        heights = jnp.exp(jax.random.uniform(jax.random.fold_in(own, axis_at), (parts,), jnp.float32, least / len(split), largest / len(split)))
        loudness = loudness * jnp.repeat(heights, shape[axis_at] // parts).reshape([-1 if axis == axis_at else 1 for axis in range(len(shape))])
    return loudness


def assign_block(key, own, number, rows, number_of, top, bound, skew):
    order = jax.random.permutation(key, number_of)
    crowded, common = load_shares(number_of, rows * top, bound, skew, True), load_shares(number_of, rows * top, bound, skew, False)
    places = jnp.arange(number_of)

    def named(tallies, turn):
        used = int((tallies > 0).sum())
        fixed = max(1, used // 4)
        moved = fixed + (places - fixed + turn * (used - fixed)) % max(1, number_of - fixed)
        return jnp.zeros((number_of,), jnp.int32).at[order[jnp.where(places < fixed, places, moved)]].set(jnp.asarray(tallies, jnp.int32))

    tallies = jnp.where(number % 4 == 0, named(crowded, number // 4), named(common, number - number // 4 - 1))
    mixed = jax.random.permutation(jax.random.fold_in(own, 3), number_of)
    giver, taker = mixed[0:number_of // 2 * 2:2], mixed[1:number_of // 2 * 2:2]
    slack = jnp.minimum(tallies[giver] - 1, bound - tallies[taker]) // 2
    slack = jnp.where((giver == order[0]) | (taker == order[0]) | (tallies[taker] == 0), 0, jnp.maximum(slack, 0))
    moved = jax.random.randint(jax.random.fold_in(own, 4), (number_of // 2,), 0, 1 << 20) % (slack + 1)
    tallies = tallies.at[giver].add(-moved).at[taker].add(moved)
    members = jnp.searchsorted(jnp.cumsum(tallies), jnp.arange(rows * top), side="right").astype(jnp.int32)
    listing = members.reshape(top, rows).T
    listing = listing[jax.random.permutation(jax.random.fold_in(own, 1), rows)]
    turn = jax.random.randint(jax.random.fold_in(own, 2), (rows, 1), 0, top)
    return jnp.take_along_axis(listing, (jnp.arange(top)[None, :] + turn) % top, axis=1)


def load_shares(count, total, bound, slope, full):
    weights = [(1 << 20) // math.isqrt(grade ** slope) + 1 for grade in range(1, count + 1)]
    largest = bound if full else min(bound, max(-(-total // count), total * weights[0] // sum(weights)))
    least = 1 if total - largest >= count - 1 else 0
    given, rest = [largest] + [least] * (count - 1), total - largest - least * (count - 1)
    while rest > 0:
        movable = [i for i in range(1, count) if given[i] < largest] or [i for i in range(1, count) if given[i] < bound]
        whole, left = sum([weights[i] for i in movable]), rest
        for i in movable:
            addition = min(bound - given[i], max(1, left * weights[i] // whole), rest)
            given[i] = given[i] + addition
            rest = rest - addition
    return np.array(given)


def centred(stream_key, shape, deviation, limit, cuts=(), held_as=jnp.bfloat16):
    values = deviation * jax.random.normal(stream_key, shape, jnp.float32)
    if cuts:
        values = values * steps_of(stream_key, shape, cuts, -0.22, 0.18)
    return jnp.clip(values, -limit, limit).astype(held_as)


def setup_inputs(seed: int = 0, part: int = 0) -> dict:
    seeds = jax.random.split(jax.random.key(seed), 12)
    part_keys = jax.random.split(jax.random.fold_in(seeds[11], part), 12)
    query_rows = draw_query_rows(jax.random.fold_in(jax.random.fold_in(seeds[11], part), 71), part)
    key_rows = draw_key_rows(jax.random.fold_in(jax.random.fold_in(seeds[11], part), 71), part)
    value_rows = centred(part_keys[2], (SEQS, SEQ_LEN, KVH * HD), 1.0, 6.0, ((0, 4), (1, 4)))
    residual_in = centred(part_keys[3], (SEQS, SEQ_LEN, D), 1.0, 6.0, ((0, 4), (1, 4)))
    out_proj = centred(seeds[4], (QH * HD, D), HD ** -0.5, 0.5, ((0, 4),))
    norm_gain = jnp.clip(1.0 + 0.18 * jax.random.normal(seeds[5], (D,), jnp.float32), 0.099609375, 1.8984375).astype(jnp.bfloat16)
    expert_ids_keys = jax.random.split(jax.random.fold_in(part_keys[6], 1), SEQS * SEQ_LEN // TOK_DEV)
    expert_ids_turns = jax.random.permutation(jax.random.fold_in(part_keys[6], 3), SEQS * SEQ_LEN // TOK_DEV)
    expert_ids = jax.vmap(lambda own, number: assign_block(jax.random.fold_in(part_keys[6], 2), own, number, TOK_DEV, EXPERTS, TOPK, CAP, 2))(expert_ids_keys, expert_ids_turns).reshape((SEQS, SEQ_LEN, TOPK))
    gate_weights = jnp.clip(jnp.exp(math.log(1.0) - 2.9996462 * jax.random.uniform(part_keys[7], (SEQS, SEQ_LEN, TOPK), jnp.float32) ** steps_of(part_keys[7], (SEQS, SEQ_LEN, TOPK), ((0, 4), (1, 4)), -0.2, 0.2)), 0.049804688, 1.0).astype(jnp.bfloat16)
    expert_gate = centred(seeds[8], (EXPERTS, D, FF), D ** -0.5, 0.125, ((0, 16),))
    expert_up = centred(seeds[9], (EXPERTS, D, FF), D ** -0.5, 0.125, ((0, 16),))
    expert_down = centred(seeds[10], (EXPERTS, FF, D), FF ** -0.5, 0.21875, ((0, 16),))
    return {"query_rows": query_rows, "key_rows": key_rows, "value_rows": value_rows, "residual_in": residual_in, "out_proj": out_proj, "norm_gain": norm_gain, "expert_ids": expert_ids, "gate_weights": gate_weights, "expert_gate": expert_gate, "expert_up": expert_up, "expert_down": expert_down}


def reference(query_rows, key_rows, value_rows, residual_in, out_proj, norm_gain, expert_ids, gate_weights, expert_gate, expert_up, expert_down):
    group = QH // KVH
    scale = 1.0 / HD ** 0.5
    length = SEQ_LEN
    query_heads = query_rows.reshape(SEQS, length, QH, HD).transpose(0, 2, 1, 3).reshape(SEQS * QH, length, HD)
    key_heads = key_rows.reshape(SEQS, length, KVH, HD).transpose(0, 2, 1, 3)
    value_heads = value_rows.reshape(SEQS, length, KVH, HD).transpose(0, 2, 1, 3)
    positions = jnp.arange(length, dtype=jnp.int32)
    causal = positions[:, None] >= positions[None, :]

    def one_head(index):
        seq_index = index // QH
        kv_index = index % QH // group
        scores = jnp.dot(query_heads[index].astype(jnp.float32), key_heads[seq_index, kv_index].astype(jnp.float32).T, precision=lax.Precision.HIGHEST) * scale
        scores = jnp.where(causal, scores, -1e+30)
        peak = lax.optimization_barrier(jnp.max(scores, axis=1, keepdims=True))
        weights = jnp.exp(scores - peak)
        probs = (weights / lax.optimization_barrier(jnp.sum(weights, axis=1, keepdims=True))).astype(jnp.bfloat16)
        probs = lax.optimization_barrier(probs)
        return jnp.dot(probs.astype(jnp.float32), value_heads[seq_index, kv_index].astype(jnp.float32), precision=lax.Precision.HIGHEST).astype(jnp.bfloat16)
    head_out = lax.map(one_head, jnp.arange(SEQS * QH, dtype=jnp.int32))
    attended = head_out.reshape(SEQS, QH, length, HD).transpose(0, 2, 1, 3).reshape(SEQS * length, QH * HD)
    projected = jnp.dot(attended, out_proj, preferred_element_type=jnp.float32)
    hidden = (residual_in.reshape(SEQS * length, D).astype(jnp.float32) + projected).astype(jnp.bfloat16)
    wide = hidden.astype(jnp.float32)
    normed = (wide * lax.rsqrt(lax.optimization_barrier(jnp.mean(wide * wide, axis=1, keepdims=True)) + 1e-06) * norm_gain.astype(jnp.float32)).astype(jnp.bfloat16)
    rows = SEQS * length
    flat_ids = expert_ids.reshape(-1).astype(jnp.int32)
    assigned = flat_ids.shape[0]
    flat_gates = gate_weights.reshape(-1)
    order = jnp.argsort(flat_ids, stable=True).astype(jnp.int32)
    sorted_ids = flat_ids[order]
    counts = jnp.zeros((EXPERTS,), jnp.int32).at[flat_ids].add(1)
    tiles = (counts + 127) // 128
    tile_end = jnp.cumsum(tiles).astype(jnp.int32)
    tile_first = tile_end - tiles
    row_first = (jnp.cumsum(counts) - counts).astype(jnp.int32)
    position = tile_first[sorted_ids] * 128 + jnp.arange(assigned, dtype=jnp.int32) - row_first[sorted_ids]
    n_tiles = assigned // 128 + EXPERTS
    slot_item = jnp.full((n_tiles * 128,), assigned, jnp.int32).at[position].set(order)
    tile_index = jnp.arange(n_tiles, dtype=jnp.int32)
    tile_owner = jnp.minimum(lax.optimization_barrier(jnp.sum((tile_end[None, :] <= tile_index[:, None]).astype(jnp.int32), axis=1)), EXPERTS - 1)
    padded_rows = jnp.concatenate([normed, jnp.zeros((1, D), jnp.bfloat16)], axis=0)
    padded_gates = jnp.concatenate([flat_gates, jnp.zeros((1,), jnp.bfloat16)], axis=0)
    slot_token = jnp.where(slot_item < assigned, slot_item // TOPK, rows).astype(jnp.int32)

    def tile_step(total, tile):
        owner = tile_owner[tile]
        tokens_here = lax.dynamic_slice_in_dim(slot_token, tile * 128, 128)
        items = lax.dynamic_slice_in_dim(slot_item, tile * 128, 128)
        inputs = padded_rows[tokens_here].astype(jnp.float32)
        gate_proj = jnp.dot(inputs, expert_gate[owner].astype(jnp.float32), precision=lax.Precision.HIGHEST)
        up_proj = jnp.dot(inputs, expert_up[owner].astype(jnp.float32), precision=lax.Precision.HIGHEST)
        inner = lax.optimization_barrier((jax.nn.silu(gate_proj) * up_proj).astype(jnp.bfloat16))
        result = jnp.dot(inner.astype(jnp.float32), expert_down[owner].astype(jnp.float32), precision=lax.Precision.HIGHEST)
        result = result * padded_gates[items].astype(jnp.float32)[:, None]
        rounded = lax.optimization_barrier(result.astype(jnp.bfloat16))
        return (total.at[tokens_here].add(rounded.astype(jnp.float32)), None)
    total, _ = lax.scan(tile_step, jnp.zeros((rows + 1, D), jnp.float32), tile_index)
    layer_out = (wide + total[:rows]).astype(jnp.bfloat16)
    return layer_out.reshape(SEQS, length, D)
```

```python
import functools
import jax
import jax.numpy as jnp
from jax import lax
from jax.experimental import pallas as pl
from jax.experimental.pallas import tpu as pltpu
from jax.sharding import PartitionSpec as P

D = 2048
HD = 128
QH = 16
KVH = 2


def attend_head(queries, keys_one, values_one, block):
    length = queries.shape[0]
    scale = 1.0 / queries.shape[1] ** 0.5
    pieces = []
    for part_index in range(length // block):
        stop = (part_index + 1) * block
        rows_here = queries[part_index * block : stop]
        scores = (
            jnp.einsum("qd,kd->qk", rows_here, keys_one[:stop], preferred_element_type=jnp.float32)
            * scale
        )
        row_pos = part_index * block + jnp.arange(block, dtype=jnp.int32)
        col_pos = jnp.arange(stop, dtype=jnp.int32)
        scores = jnp.where(row_pos[:, None] >= col_pos[None, :], scores, -1e30)
        peak = jnp.max(scores, axis=1, keepdims=True)
        weights = jnp.exp(scores - peak)
        probs = (weights / jnp.sum(weights, axis=1, keepdims=True)).astype(jnp.bfloat16)
        pieces.append(
            jnp.dot(probs, values_one[:stop], preferred_element_type=jnp.float32).astype(
                jnp.bfloat16
            )
        )
    return jnp.concatenate(pieces, axis=0)


def rank_in_expert(flat_ids, experts):
    items = flat_ids.shape[0]
    width = 128
    n_parts = items // width
    onehot = (
        (flat_ids[:, None] == jnp.arange(experts, dtype=jnp.int32)[None, :])
        .astype(jnp.bfloat16)
        .reshape(n_parts, width, experts)
    )
    lower = (
        jnp.arange(width, dtype=jnp.int32)[:, None] > jnp.arange(width, dtype=jnp.int32)[None, :]
    ).astype(jnp.bfloat16)
    within = jnp.einsum("ij,bje->bie", lower, onehot, preferred_element_type=jnp.float32)
    part_counts = jnp.sum(onehot.astype(jnp.float32), axis=1)
    earlier = jnp.cumsum(part_counts, axis=0) - part_counts
    ranks = jnp.sum((within + earlier[:, None, :]) * onehot.astype(jnp.float32), axis=2)
    return ranks.reshape(items).astype(jnp.int32)


def per_device_routed(
    query_rows,
    key_rows,
    value_rows,
    residual_in,
    out_proj,
    norm_gain,
    expert_ids,
    gate_weights,
    expert_gate,
    expert_up,
    expert_down,
):
    tokens = query_rows.shape[1]
    n_seq = lax.axis_size("seq")
    n_sub = lax.axis_size("sub")
    heads_here = QH // n_seq
    group = QH // KVH
    query_local = lax.all_to_all(query_rows, "seq", split_axis=2, concat_axis=1, tiled=True)
    key_full, value_full = (
        lax.all_gather(key_rows, "seq", axis=1, tiled=True),
        lax.all_gather(value_rows, "seq", axis=1, tiled=True),
    )
    first_head = lax.axis_index("seq") * heads_here
    key_list = []
    value_list = []
    for head in range(heads_here):
        kv_start = (first_head + head) // group * HD
        key_list.append(lax.dynamic_slice_in_dim(key_full[0], kv_start, HD, 1))
        value_list.append(lax.dynamic_slice_in_dim(value_full[0], kv_start, HD, 1))
    length = query_local.shape[1]
    block = min(length, max(512, length // 8))
    outputs = [
        attend_head(
            query_local[0, :, head * HD : (head + 1) * HD], key_list[head], value_list[head], block
        )
        for head in range(heads_here)
    ]
    head_block = jnp.concatenate(outputs, axis=1)[None]
    attended = lax.all_to_all(head_block, "seq", split_axis=1, concat_axis=2, tiled=True)[0]
    projected = jnp.dot(
        attended,
        lax.all_gather(out_proj, "seq", axis=0, tiled=True),
        preferred_element_type=jnp.float32,
    )
    hidden = (residual_in[0].astype(jnp.float32) + projected).astype(jnp.bfloat16)
    wide = hidden.astype(jnp.float32)
    normed = (
        wide
        * lax.rsqrt(jnp.mean(wide * wide, axis=1, keepdims=True) + 1e-06)
        * norm_gain.astype(jnp.float32)
    ).astype(jnp.bfloat16)
    topk = expert_ids.shape[2]
    experts = n_seq * n_sub
    cap = max(2, (5 * tokens * topk + 4 * experts - 1) // (4 * experts))
    flat_ids = expert_ids[0].reshape(-1)
    items = flat_ids.shape[0]
    ranks = rank_in_expert(flat_ids, experts)
    slot_of = flat_ids * cap + ranks
    slots_out = experts * cap
    item_of_slot = (
        jnp.full((slots_out,), items, jnp.int32).at[slot_of].set(jnp.arange(items, dtype=jnp.int32))
    )
    padded_rows = jnp.concatenate([normed, jnp.zeros((1, D), jnp.bfloat16)], axis=0)
    padded_gates = jnp.concatenate(
        [gate_weights[0].reshape(-1), jnp.zeros((1,), jnp.bfloat16)], axis=0
    )
    token_of_slot = jnp.where(item_of_slot < items, item_of_slot // topk, tokens)
    send_rows = padded_rows[token_of_slot].reshape(experts, cap, D)
    send_gates = padded_gates[item_of_slot].reshape(experts, cap)
    recv_rows, recv_gates = (
        lax.all_to_all(send_rows, ("seq", "sub"), split_axis=0, concat_axis=0, tiled=True),
        lax.all_to_all(send_gates, ("seq", "sub"), split_axis=0, concat_axis=0, tiled=True),
    )
    slots_in = experts * cap
    valid = recv_gates > 0
    counts = jnp.sum(valid.astype(jnp.int32), axis=1)
    offsets = jnp.cumsum(counts) - counts
    dest = jnp.where(
        valid, offsets[:, None] + jnp.arange(cap, dtype=jnp.int32)[None, :], slots_in
    ).reshape(-1)
    source_of = (
        jnp.full((slots_in + 1,), slots_in, jnp.int32)
        .at[dest]
        .set(jnp.arange(slots_in, dtype=jnp.int32))[:slots_in]
    )
    compact_rows = jnp.concatenate(
        [recv_rows.reshape(slots_in, D), jnp.zeros((1, D), jnp.bfloat16)], axis=0
    )[source_of]
    compact_gates = jnp.concatenate(
        [recv_gates.reshape(-1), jnp.zeros((1,), jnp.bfloat16)], axis=0
    )[source_of].astype(jnp.float32)
    filled = jnp.sum(counts)
    n_blocks = (filled + slots_in - 1) // slots_in
    w_gate = expert_gate[0]
    w_up = expert_up[0]
    w_down = expert_down[0]

    def expert_block(index, results):
        gate_proj = jnp.dot(compact_rows, w_gate, preferred_element_type=jnp.float32)
        up_proj = jnp.dot(compact_rows, w_up, preferred_element_type=jnp.float32)
        inner = (jax.nn.silu(gate_proj) * up_proj).astype(jnp.bfloat16)
        weighted = (
            jnp.dot(inner, w_down, preferred_element_type=jnp.float32) * compact_gates[:, None]
        )
        return weighted.astype(jnp.bfloat16)

    results = lax.fori_loop(0, n_blocks, expert_block, jnp.zeros((slots_in, D), jnp.bfloat16))
    returned = jnp.concatenate([results, jnp.zeros((1, D), jnp.bfloat16)], axis=0)[dest].reshape(
        experts, cap, D
    )
    back = lax.all_to_all(
        returned, ("seq", "sub"), split_axis=0, concat_axis=0, tiled=True
    ).reshape(slots_out, D)
    gathered = back[slot_of].reshape(tokens, topk, D).astype(jnp.float32)
    mixture = jnp.sum(gathered, axis=1)
    return (wide + mixture).astype(jnp.bfloat16)[None]


def lookup(table, i, j):
    total = 0
    for a, row in enumerate(table):
        for b, value in enumerate(row):
            if value:
                hit = jnp.logical_and(i == a, j == b)
                total = total + jnp.where(hit, value, 0)
    return total


def gather_tables(n):
    arrivals, chunks = [], []
    for z in range(n):
        mate = z + 1 - 2 * (z % 2)
        here = [(z, 0), (z, 1)]
        for step in range(2 * n):
            j, h = step // 2, step % 2
            for p in (z - 1 - j, z + 1 + j):
                if 0 <= p < n and not (p == mate and h == 1):
                    here.append((p, h))
        arrivals.append([2 * p + h for p, h in here])
        ready = {}
        for p in range(n):
            if p != z:
                ready[(p, 0)] = 2 * (abs(p - z) - 1) + 1
            last = max(i for i, (q, _) in enumerate(here) if q == p)
            ready[(p, 1)] = max(last, (2 * n - 2 if mate_step(n, z) > 3 else 3) if p == mate else 0)
        order, left = [], sorted(ready, key=lambda item: (ready[item], item[0] == mate, item))
        for step in range(1, 2 * n):
            item = left.pop(0)
            assert ready[item] <= step
            order.append(2 * item[0] + item[1])
        chunks.append(order)
    return arrivals, chunks


def mate_step(n, z):
    mate = z + 1 - 2 * (z % 2)
    corner = z == 0 or z == n - 1
    return 2 * n - 2 if corner else 3


def return_tables(n):
    across = [[(2, 0), (3, 0), (3, 1), (2, 1), (1, 0), (0, 0)], [(0, 0), (2, 0), (3, 0), (3, 1), (2, 1), (1, 0)]]
    along = [
        [(1, 1), (2, 0), (3, 0), (3, 1), (2, 1), (1, 0), (0, 0), (0, 1)],
        [(2, 0), (3, 0), (0, 0), (3, 1), (2, 1), (0, 1), (1, 0), (1, 1)],
    ]
    pick = lambda rows: [[2 * p + h for p, h in row] for row in rows] + [
        [2 * (n - 1 - p) + h for p, h in row] for row in reversed(rows)
    ]
    return pick(across), pick(along)


def first_uses(rows):
    return [[int(v // 2 not in [u // 2 for u in row[:i]]) for i, v in enumerate(row)] for row in rows]


def layer_kernel(
    n_sub,
    q_hbm,
    k_hbm,
    v_hbm,
    residual_hbm,
    proj_hbm,
    gain_ref,
    ids_ref,
    gates_ref,
    wg_hbm,
    wu_hbm,
    wd_hbm,
    o_ref,
    q_all,
    k_all,
    v_all,
    proj,
    residual,
    partial,
    core_far,
    core_near,
    across_near,
    wide_ref,
    q_send,
    q_recv,
    kv_send,
    kv_recv,
    part_send,
    part_recv,
    coef,
    coef_send,
    coef_recv,
    coef_up,
    coef_down,
    coef_z,
    rows,
    outs,
    from_core,
    from_y,
    from_low,
    from_high,
    from_mate,
    wg,
    wu,
    wd,
    load_sem,
    row_recv,
    up_send,
    down_send,
    y_send,
    core_send,
    relay_send,
    core_recv,
    result_send,
    y_recv,
    result_y_send,
    low_recv,
    high_recv,
    result_up_send,
    result_down_send,
    mate_send,
    mate_recv,
):
    seq = lax.axis_index("seq")
    z = lax.axis_index("sub")
    y = seq // 2
    c = seq % 2
    tokens = residual.shape[0]
    share = q_all.shape[1]
    heads = share // HD
    length = q_all.shape[0]
    group = QH // KVH
    half = tokens // 2
    me = seq * n_sub + z
    tile = coef.shape[0] // (4 * n_sub)
    y_order, chunk_order = gather_tables(n_sub)
    across_order, along_order = return_tables(n_sub)
    high = {"sub": z + 1}
    low = {"sub": z - 1}
    across = {"seq": (1 - y) * 2 + c}
    partner = {"seq": y * 2 + 1 - c}
    diagonal = {"seq": (1 - y) * 2 + 1 - c}
    mate = z + 1 - 2 * (z % 2)
    beside = {"sub": mate}
    has_high = z < n_sub - 1
    has_low = z > 0
    corner = jnp.logical_not(jnp.logical_and(has_low, has_high))

    def slot(yy, p, cc):
        return (yy * n_sub + p) * 2 + cc

    def piece(ref, index, h):
        return ref.at[pl.ds(pl.multiple_of(index * tokens + h * half, half), half), :]

    def remote(src, dst, send, recv, target):
        return pltpu.make_async_remote_copy(
            src_ref=src,
            dst_ref=dst,
            send_sem=send,
            recv_sem=recv,
            device_id=target,
            device_id_type=pl.DeviceIdType.MESH,
        )

    def guarded(condition, action):
        if condition is None:
            action()
        else:
            pl.when(condition)(action)

    def query_part(s):
        return q_hbm.at[:, pl.ds(pl.multiple_of(s * share, share), share)]

    def cache_part(ref, s):
        return ref.at[:, pl.ds(pl.multiple_of(s * heads // group * HD, HD), HD)]

    def token_rows(ref, s):
        return ref.at[pl.ds(pl.multiple_of(s * tokens, tokens), tokens), :]

    barrier = pltpu.get_barrier_semaphore()
    for peer in (across, partner, diagonal):
        pl.semaphore_signal(barrier, 1, device_id=peer, device_id_type=pl.DeviceIdType.MESH)

    @pl.when(has_high)
    def _():
        pl.semaphore_signal(barrier, 1, device_id=high, device_id_type=pl.DeviceIdType.MESH)

    @pl.when(has_low)
    def _():
        pl.semaphore_signal(barrier, 1, device_id=low, device_id_type=pl.DeviceIdType.MESH)

    own_parts = [
        pltpu.make_async_copy(query_part(seq), token_rows(q_all, seq), load_sem.at[0]),
        pltpu.make_async_copy(cache_part(k_hbm, seq), token_rows(k_all, seq), load_sem.at[1]),
        pltpu.make_async_copy(cache_part(v_hbm, seq), token_rows(v_all, seq), load_sem.at[2]),
        pltpu.make_async_copy(proj_hbm, proj, load_sem.at[3]),
    ]
    loads = [
        pltpu.make_async_copy(residual_hbm, residual, load_sem.at[7]),
        pltpu.make_async_copy(wg_hbm, wg, load_sem.at[4]),
        pltpu.make_async_copy(wu_hbm, wu, load_sem.at[5]),
        pltpu.make_async_copy(wd_hbm, wd, load_sem.at[6]),
    ]
    for load in own_parts + loads:
        load.start()

    lanes = 128 * ((4 * n_sub + 127) // 128)
    lane = lax.broadcasted_iota(jnp.int32, (tokens, lanes), 1)
    ids = ids_ref[...]
    gates = gates_ref[...].astype(jnp.float32)
    weights_here = jnp.zeros((tokens, lanes), jnp.float32)
    for k in range(ids.shape[1]):
        weights_here = weights_here + jnp.where(ids[:, k : k + 1] == lane, gates[:, k : k + 1], 0.0)
    identity = (
        lax.broadcasted_iota(jnp.int32, (tokens, tokens), 0)
        == lax.broadcasted_iota(jnp.int32, (tokens, tokens), 1)
    ).astype(jnp.float32).astype(jnp.bfloat16)
    turned = lax.dot_general(
        weights_here.astype(jnp.bfloat16),
        identity,
        (((0,), (0,)), ((), ())),
        preferred_element_type=jnp.float32,
    )

    def coef_tile(p, s, count=1):
        return pl.ds(pl.multiple_of((p * 4 + s) * tile, tile), count * tile)

    coef[coef_tile(z, seq), :] = turned[:tile].astype(jnp.bfloat16)

    peers = 3 + jnp.where(has_high, 1, 0) + jnp.where(has_low, 1, 0)
    with jax.named_scope("BAR"):
        pl.semaphore_wait(barrier, peers)

    others = (
        ((1 - y) * 2 + c, across),
        ((1 - y) * 2 + 1 - c, diagonal),
        (y * 2 + 1 - c, partner),
    )

    def scatter_copies(s, target):
        return (
            remote(
                cache_part(k_hbm, s),
                token_rows(k_all, seq),
                kv_send.at[s],
                kv_recv.at[seq],
                target,
            ),
            remote(
                cache_part(v_hbm, s),
                token_rows(v_all, seq),
                kv_send.at[4 + s],
                kv_recv.at[4 + seq],
                target,
            ),
            remote(
                query_part(s), token_rows(q_all, seq), q_send.at[s], q_recv.at[seq], target
            ),
        )

    def coef_near(s, target):
        here = coef.at[coef_tile(z, seq), :]
        return remote(here, here, coef_send.at[s], coef_recv.at[seq], target)

    for s, target in others:
        for copy in scatter_copies(s, target):
            copy.start()
    for s, target in others:
        coef_near(s, target).start()

    def arrival(ref, s, sem):
        return remote(token_rows(ref, s), token_rows(ref, s), q_send.at[s], sem, partner)

    def coef_hop(p, send, target):
        here = coef.at[coef_tile(p, 0, 4), :]
        return remote(here, here, send.at[p], coef_z.at[p], target)

    def coef_take(p, way):
        coef_hop(p, coef_up, high).wait_recv()

        @pl.when(has_high if way > 0 else has_low)
        def _():
            (coef_hop(p, coef_up, high) if way > 0 else coef_hop(p, coef_down, low)).start()

    def coef_step(d):
        pl.when(z - d >= 0)(lambda: coef_take(z - d, 1))
        pl.when(z + d < n_sub)(lambda: coef_take(z + d, -1))

    for load in own_parts:
        load.wait()
    with jax.named_scope("ARR"):
        for s, _ in others:
            arrival(k_all, s, kv_recv.at[s]).wait_recv()
            arrival(v_all, s, kv_recv.at[4 + s]).wait_recv()
            arrival(q_all, s, q_recv.at[s]).wait_recv()

    for s, target in others:
        there = coef.at[coef_tile(z, s), :]
        remote(there, there, coef_send.at[s], coef_recv.at[s], target).wait_recv()
    pl.when(has_high)(lambda: coef_hop(z, coef_up, high).start())
    pl.when(has_low)(lambda: coef_hop(z, coef_down, low).start())

    far_copy = remote(
        token_rows(partial, (1 - y) * 2 + 1 - c), core_far, part_send.at[0], part_recv.at[0], partner
    )
    across_copy = remote(
        token_rows(partial, (1 - y) * 2 + c),
        across_near,
        part_send.at[1],
        part_recv.at[1],
        across,
    )
    near_copy = remote(
        token_rows(partial, y * 2 + 1 - c), core_near, part_send.at[2], part_recv.at[2], partner
    )

    def attend_step(j, carry):
        yy = jnp.where(j < 2, 1 - y, y)
        cc = jnp.where(j % 2 == 0, 1 - c, c)
        i = yy * 2 + cc
        at = pl.ds(pl.multiple_of(i * tokens, tokens), tokens)
        row_pos = i * tokens + lax.broadcasted_iota(jnp.int32, (tokens, length), 0)
        col_pos = lax.broadcasted_iota(jnp.int32, (tokens, length), 1)
        allowed = row_pos >= col_pos
        outputs = []
        for head in range(heads):
            scores = lax.dot_general(
                q_all[at, head * HD : (head + 1) * HD],
                k_all[...],
                (((1,), (1,)), ((), ())),
                preferred_element_type=jnp.float32,
            ) * (1.0 / HD**0.5)
            scores = jnp.where(allowed, scores, -1e30)
            weights = jnp.exp(scores - jnp.max(scores, axis=1, keepdims=True))
            total = jnp.sum(weights, axis=1, keepdims=True)
            probs = (weights * (1.0 / total)).astype(jnp.bfloat16)
            outputs.append(
                jnp.dot(probs, v_all[...], preferred_element_type=jnp.float32).astype(jnp.bfloat16)
            )
        projected = jnp.dot(
            jnp.concatenate(outputs, axis=1), proj[...], preferred_element_type=jnp.float32
        )

        @pl.when(j != 1)
        def _():
            partial[at, :] = projected.astype(jnp.bfloat16)

        @pl.when(j == 0)
        def _():
            far_copy.start()

        @pl.when(j == 1)
        def _():
            far_copy.wait_recv()
            partial[at, :] = (projected + core_far[...].astype(jnp.float32)).astype(jnp.bfloat16)
            across_copy.start()

        @pl.when(j == 2)
        def _():
            near_copy.start()

        return carry

    with jax.named_scope("ATT"):
        lax.fori_loop(0, 4, attend_step, 0)
    coef_step(1)
    for load in loads:
        load.wait()
    near_copy.wait_recv()
    own_rows = pl.ds(pl.multiple_of(seq * tokens, tokens), tokens)
    base = (
        residual[...].astype(jnp.float32)
        + partial[own_rows, :].astype(jnp.float32)
        + core_near[...].astype(jnp.float32)
    )
    with jax.named_scope("ACR"):
        across_copy.wait_recv()
    hidden = (base + across_near[...].astype(jnp.float32)).astype(jnp.bfloat16)
    wide_ref[...] = hidden
    wide = hidden.astype(jnp.float32)
    normed = (
        wide
        * lax.rsqrt(jnp.mean(wide * wide, axis=1, keepdims=True) + 1e-06)
        * gain_ref[...].astype(jnp.float32)[None, :]
    ).astype(jnp.bfloat16)
    own_slot = pl.ds(pl.multiple_of(slot(y, z, c) * tokens, tokens), tokens)
    rows[own_slot, :] = normed

    def row_copy(index, h, send, target):
        here = piece(rows, index, h)
        return remote(here, here, send, row_recv.at[index * 2 + h], target)

    def wait_rows(index, h):
        row_copy(index, h, relay_send.at[0], partner).wait_recv()

    def column_copies(p, h):
        index = slot(y, p, c)
        at = p * 2 + h
        return (
            (jnp.logical_and(p <= z, has_high), row_copy(index, h, up_send.at[at], high)),
            (jnp.logical_and(p >= z, has_low), row_copy(index, h, down_send.at[at], low)),
            (
                jnp.logical_or(p != mate, h == 0),
                row_copy(index, h, y_send.at[at], across),
            ),
            (None, row_copy(index, h, core_send.at[at], partner)),
        )

    def spread(p, h):
        for condition, copy in column_copies(p, h):
            guarded(condition, copy.start)

    def relay_copy(p, h):
        return row_copy(slot(1 - y, p, c), h, relay_send.at[p * 2 + h], partner)

    def result_copy(yy, p):
        index = slot(yy, p, 1 - c)
        pair = yy * n_sub + p
        src = outs.at[pl.ds(pl.multiple_of(index * tokens, tokens), tokens), :]
        dst = from_core.at[pl.ds(pl.multiple_of(pair * tokens, tokens), tokens), :]
        return remote(src, dst, result_send.at[pair], core_recv.at[pair], partner)

    mine = (
        lax.broadcasted_iota(jnp.int32, (2 * tile, 128), 0) % tile == me
    ).astype(jnp.float32).astype(jnp.bfloat16)

    def compute(yy, p):
        wait_rows(slot(yy, p, 1 - c), 0)
        wait_rows(slot(yy, p, 1 - c), 1)
        with jax.named_scope("C"):
            at = pl.ds(pl.multiple_of((yy * n_sub + p) * 2 * tokens, 2 * tokens), 2 * tokens)
            x = rows[at, :]
            gains = [
                lax.dot_general(
                    coef[coef_tile(p, 2 * yy + cc), :],
                    mine[:tile],
                    (((0,), (0,)), ((), ())),
                    preferred_element_type=jnp.float32,
                )
                for cc in range(2)
            ]
            coeff = jnp.concatenate(gains, axis=0)[:, :1]
            gate = jnp.dot(x, wg[...], preferred_element_type=jnp.float32)
            up = jnp.dot(x, wu[...], preferred_element_type=jnp.float32)
            inner = (gate / (1.0 + jnp.exp(-gate)) * up).astype(jnp.bfloat16)
            out = jnp.dot(inner, wd[...], preferred_element_type=jnp.float32)
            outs[at, :] = (out * coeff).astype(jnp.bfloat16)
        result_copy(yy, p).start()

    def mate_rows():
        return row_copy(slot(1 - y, z, c), 1, mate_send.at[0], beside)

    spread(z, 0)
    spread(z, 1)
    coef_step(2)
    compute(y, z)

    def take(p, h):
        wait_rows(slot(y, p, c), h)
        spread(p, h)

    def compute_next(k):
        chunk = lookup(chunk_order, z, k)
        compute(jnp.where(chunk % 2 == 1, 1 - y, y), chunk // 2)

    steps = 2 * n_sub - 1

    def gather_step(k, carry):
        h = k % 2
        below = z - 1 - k // 2
        above = z + 1 + k // 2
        pl.when(below >= 0)(lambda: take(below, h))
        pl.when(above < n_sub)(lambda: take(above, h))
        which = lookup(y_order, z, k)
        wait_rows(slot(1 - y, which // 2, c), which % 2)
        relay_copy(which // 2, which % 2).start()

        @pl.when(k == jnp.where(corner, 1, 3))
        def _():
            mate_rows().start()

        @pl.when(k == jnp.where(corner, steps - 1, 3))
        def _():
            wait_rows(slot(1 - y, mate, c), 1)
            relay_copy(mate, 1).start()

        @pl.when(k == 1)
        def _():
            coef_step(3)

        @pl.when(jnp.logical_and(k > 0, k < steps - 1))
        def _():
            compute_next(k - 1)

        return carry

    with jax.named_scope("GATHER"):
        lax.fori_loop(0, steps, gather_step, 0)

    def wide_load(ref, index, h):
        at = pl.ds(pl.multiple_of(index * tokens + h * half, half), half)
        return ref[at, :].astype(jnp.float32)

    def y_copy(p, h):
        at = p * 2 + h
        return remote(
            piece(outs, slot(1 - y, p, c), h),
            piece(from_y, p, h),
            result_y_send.at[at],
            y_recv.at[at],
            across,
        )

    def z_copy(p, h, buffer, send, recv, target):
        at = p * 2 + h
        return remote(
            piece(outs, slot(y, p, c), h), piece(buffer, p, h), send.at[at], recv.at[at], target
        )

    def up_copy(p, h):
        return z_copy(p, h, from_low, result_up_send, low_recv, high)

    def down_copy(p, h):
        return z_copy(p, h, from_high, result_down_send, high_recv, low)

    def store_out(index, h, value):
        at = pl.ds(pl.multiple_of(index * tokens + h * half, half), half)
        outs[at, :] = value.astype(jnp.bfloat16)

    def mate_result(p):
        return remote(
            piece(outs, slot(1 - y, p, c), 1), from_mate, mate_send.at[1], mate_recv.at[0], beside
        )

    def chip_sum(yy, p, h):
        index = slot(yy, p, c)
        store_out(index, h, wide_load(outs, index, h) + wide_load(from_core, yy * n_sub + p, h))

    across_first = first_uses(across_order)
    along_first = first_uses(along_order)

    def send_across(k):
        which = lookup(across_order, z, k)
        p, h = which // 2, which % 2
        pl.when(lookup(across_first, z, k) == 1)(lambda: result_copy(1 - y, p).wait_recv())
        chip_sum(1 - y, p, h)
        y_copy(p, h).start()

    send_across(0)

    def tail_step(k, carry):
        compute_next(k)
        return carry

    lax.fori_loop(steps - 2, steps, tail_step, 0)

    def across_step(k, carry):
        send_across(k)
        return carry

    with jax.named_scope("ACROSS"):
        lax.fori_loop(1, steps - 1, across_step, 0)
        chip_sum(1 - y, mate, 1)
        mate_result(mate).start()

    def along_step(k, carry):
        which = lookup(along_order, z, k)
        p, h = which // 2, which % 2
        index = slot(y, p, c)
        direct = jnp.logical_or(p != mate, h == 0)

        @pl.when(k == jnp.where(corner, 2, 4))
        def _():
            mate_result(z).wait_recv()
            here = slot(1 - y, z, c)
            chip_sum(1 - y, z, 1)
            store_out(here, 1, wide_load(outs, here, 1) + from_mate[...].astype(jnp.float32))
            y_copy(z, 1).start()

        pl.when(lookup(along_first, z, k) == 1)(lambda: result_copy(y, p).wait_recv())
        chip_sum(y, p, h)

        @pl.when(direct)
        def _():
            y_copy(p, h).wait_recv()
            store_out(index, h, wide_load(outs, index, h) + wide_load(from_y, p, h))

        @pl.when(p > z)
        def _():
            @pl.when(has_low)
            def _():
                up_copy(p, h).wait_recv()
                store_out(index, h, wide_load(outs, index, h) + wide_load(from_low, p, h))

            up_copy(p, h).start()

        @pl.when(p < z)
        def _():
            @pl.when(has_high)
            def _():
                down_copy(p, h).wait_recv()
                store_out(index, h, wide_load(outs, index, h) + wide_load(from_high, p, h))

            down_copy(p, h).start()

        @pl.when(p == z)
        def _():
            at = pl.ds(pl.multiple_of(h * half, half), half)

            @pl.when(has_low)
            def _():
                up_copy(p, h).wait_recv()
                store_out(index, h, wide_load(outs, index, h) + wide_load(from_low, p, h))

            @pl.when(has_high)
            def _():
                down_copy(p, h).wait_recv()
                store_out(index, h, wide_load(outs, index, h) + wide_load(from_high, p, h))

            o_ref[at, :] = (wide_ref[at, :].astype(jnp.float32) + wide_load(outs, index, h)).astype(
                jnp.bfloat16
            )

        return carry

    with jax.named_scope("ALONG"):
        lax.fori_loop(0, 2 * n_sub, along_step, 0)

    def drain(k, carry):
        p = k // 2
        h = k % 2
        for condition, copy in column_copies(p, h):
            guarded(condition, copy.wait_send)

        relay_copy(p, h).wait_send()
        pl.when(jnp.logical_or(p != mate, h == 0))(lambda: y_copy(p, h).wait_send())
        result_copy(h, p).wait_send()
        pl.when(p > z)(lambda: up_copy(p, h).wait_send())
        pl.when(p < z)(lambda: down_copy(p, h).wait_send())

        @pl.when(h == 0)
        def _():
            pl.when(jnp.logical_and(p <= z, has_high))(lambda: coef_hop(p, coef_up, high).wait_send())
            pl.when(jnp.logical_and(p >= z, has_low))(lambda: coef_hop(p, coef_down, low).wait_send())

        return carry

    lax.fori_loop(0, 2 * n_sub, drain, 0)
    for s, target in others:
        for copy in scatter_copies(s, target):
            copy.wait_send()
        coef_near(s, target).wait_send()
    mate_rows().wait_send()
    mate_result(mate).wait_send()
    far_copy.wait_send()
    across_copy.wait_send()
    near_copy.wait_send()


def layer(queries, keys, values, residual, proj, gain, ids, gates, w_gate, w_up, w_down, n_sub):
    tokens, width = residual.shape
    share = proj.shape[0]
    blocks = 4 * n_sub
    tile = 16 * ((blocks + 15) // 16)
    dma = lambda count: pltpu.SemaphoreType.DMA((count,))
    hbm = pl.BlockSpec(memory_space=pl.ANY)
    vmem = pl.BlockSpec(memory_space=pltpu.VMEM)
    bf = jnp.bfloat16
    return pl.pallas_call(
        functools.partial(layer_kernel, n_sub),
        in_specs=[hbm, hbm, hbm, hbm, hbm, vmem, vmem, vmem, hbm, hbm, hbm],
        out_specs=vmem,
        out_shape=jax.ShapeDtypeStruct((tokens, width), bf),
        scratch_shapes=[
            pltpu.VMEM((4 * tokens, share), bf),
            pltpu.VMEM((4 * tokens, HD), bf),
            pltpu.VMEM((4 * tokens, HD), bf),
            pltpu.VMEM(proj.shape, bf),
            pltpu.VMEM((tokens, width), bf),
            pltpu.VMEM((4 * tokens, width), bf),
            pltpu.VMEM((tokens, width), bf),
            pltpu.VMEM((tokens, width), bf),
            pltpu.VMEM((tokens, width), bf),
            pltpu.VMEM((tokens, width), bf),
            dma(4),
            dma(4),
            dma(8),
            dma(8),
            dma(3),
            dma(3),
            pltpu.VMEM((blocks * tile, tokens), bf),
            dma(4),
            dma(4),
            dma(n_sub),
            dma(n_sub),
            dma(n_sub),
            pltpu.VMEM((blocks * tokens, width), bf),
            pltpu.VMEM((blocks * tokens, width), bf),
            pltpu.VMEM((2 * n_sub * tokens, width), bf),
            pltpu.VMEM((n_sub * tokens, width), bf),
            pltpu.VMEM((n_sub * tokens, width), bf),
            pltpu.VMEM((n_sub * tokens, width), bf),
            pltpu.VMEM((tokens // 2, width), bf),
            pltpu.VMEM(w_gate.shape, bf),
            pltpu.VMEM(w_up.shape, bf),
            pltpu.VMEM(w_down.shape, bf),
            dma(8),
            dma(2 * blocks),
            dma(2 * n_sub),
            dma(2 * n_sub),
            dma(2 * n_sub),
            dma(2 * n_sub),
            dma(2 * n_sub),
            dma(2 * n_sub),
            dma(2 * n_sub),
            dma(2 * n_sub),
            dma(2 * n_sub),
            dma(2 * n_sub),
            dma(2 * n_sub),
            dma(2 * n_sub),
            dma(2 * n_sub),
            dma(2),
            dma(1),
        ],
        compiler_params=pltpu.CompilerParams(
            collective_id=0, has_side_effects=True, vmem_limit_bytes=60 * 2**20
        ),
        name="layer",
    )(queries, keys, values, residual, proj, gain, ids, gates, w_gate, w_up, w_down)


def per_device_dense(
    query_rows,
    key_rows,
    value_rows,
    residual_in,
    out_proj,
    norm_gain,
    expert_ids,
    gate_weights,
    expert_gate,
    expert_up,
    expert_down,
):
    return layer(
        query_rows[0],
        key_rows[0],
        value_rows[0],
        residual_in[0],
        out_proj,
        norm_gain,
        expert_ids[0],
        gate_weights[0],
        expert_gate[0],
        expert_up[0],
        expert_down[0],
        lax.axis_size("sub"),
    )[None]


def per_device(*args):
    tokens = args[0].shape[1]
    topk = args[6].shape[2]
    n_seq = lax.axis_size("seq")
    experts = n_seq * lax.axis_size("sub")
    cap = max(2, (5 * tokens * topk + 4 * experts - 1) // (4 * experts))
    if 2 * cap >= tokens and n_seq == 4 and lax.axis_size("sub") == 4 and tokens == 128:
        return per_device_dense(*args)
    return per_device_routed(*args)


def solution(mesh):
    placed = (
        P(("grp", "sub"), "seq", None),
        P(("grp", "sub"), "seq", None),
        P(("grp", "sub"), "seq", None),
        P(("grp", "sub"), "seq", None),
        P("seq", None),
        P(),
        P(("grp", "sub"), "seq", None),
        P(("grp", "sub"), "seq", None),
        P(("seq", "sub"), None, None),
        P(("seq", "sub"), None, None),
        P(("seq", "sub"), None, None),
    )
    return jax.shard_map(
        per_device,
        mesh=mesh,
        in_specs=placed,
        out_specs=P(("grp", "sub"), "seq", None),
        check_vma=False,
    )
```

```python
import functools
import jax
import jax.numpy as jnp
from jax import lax
from jax.experimental import pallas as pl
from jax.experimental.pallas import tpu as pltpu
from jax.sharding import PartitionSpec as P

D = 2048
HD = 128
QH = 16
KVH = 2


def attend_head(queries, keys_one, values_one, block):
    length = queries.shape[0]
    scale = 1.0 / queries.shape[1] ** 0.5
    pieces = []
    for part_index in range(length // block):
        stop = (part_index + 1) * block
        rows_here = queries[part_index * block : stop]
        scores = (
            jnp.einsum("qd,kd->qk", rows_here, keys_one[:stop], preferred_element_type=jnp.float32)
            * scale
        )
        row_pos = part_index * block + jnp.arange(block, dtype=jnp.int32)
        col_pos = jnp.arange(stop, dtype=jnp.int32)
        scores = jnp.where(row_pos[:, None] >= col_pos[None, :], scores, -1e30)
        peak = jnp.max(scores, axis=1, keepdims=True)
        weights = jnp.exp(scores - peak)
        probs = (weights / jnp.sum(weights, axis=1, keepdims=True)).astype(jnp.bfloat16)
        pieces.append(
            jnp.dot(probs, values_one[:stop], preferred_element_type=jnp.float32).astype(
                jnp.bfloat16
            )
        )
    return jnp.concatenate(pieces, axis=0)


def rank_in_expert(flat_ids, experts):
    items = flat_ids.shape[0]
    width = 128
    n_parts = items // width
    onehot = (
        (flat_ids[:, None] == jnp.arange(experts, dtype=jnp.int32)[None, :])
        .astype(jnp.bfloat16)
        .reshape(n_parts, width, experts)
    )
    lower = (
        jnp.arange(width, dtype=jnp.int32)[:, None] > jnp.arange(width, dtype=jnp.int32)[None, :]
    ).astype(jnp.bfloat16)
    within = jnp.einsum("ij,bje->bie", lower, onehot, preferred_element_type=jnp.float32)
    part_counts = jnp.sum(onehot.astype(jnp.float32), axis=1)
    earlier = jnp.cumsum(part_counts, axis=0) - part_counts
    ranks = jnp.sum((within + earlier[:, None, :]) * onehot.astype(jnp.float32), axis=2)
    return ranks.reshape(items).astype(jnp.int32)


def per_device_routed(
    query_rows,
    key_rows,
    value_rows,
    residual_in,
    out_proj,
    norm_gain,
    expert_ids,
    gate_weights,
    expert_gate,
    expert_up,
    expert_down,
):
    tokens = query_rows.shape[1]
    n_seq = lax.axis_size("seq")
    n_sub = lax.axis_size("sub")
    heads_here = QH // n_seq
    group = QH // KVH
    query_local = lax.all_to_all(query_rows, "seq", split_axis=2, concat_axis=1, tiled=True)
    key_full, value_full = (
        lax.all_gather(key_rows, "seq", axis=1, tiled=True),
        lax.all_gather(value_rows, "seq", axis=1, tiled=True),
    )
    first_head = lax.axis_index("seq") * heads_here
    key_list = []
    value_list = []
    for head in range(heads_here):
        kv_start = (first_head + head) // group * HD
        key_list.append(lax.dynamic_slice_in_dim(key_full[0], kv_start, HD, 1))
        value_list.append(lax.dynamic_slice_in_dim(value_full[0], kv_start, HD, 1))
    length = query_local.shape[1]
    block = min(length, max(512, length // 8))
    outputs = [
        attend_head(
            query_local[0, :, head * HD : (head + 1) * HD], key_list[head], value_list[head], block
        )
        for head in range(heads_here)
    ]
    head_block = jnp.concatenate(outputs, axis=1)[None]
    attended = lax.all_to_all(head_block, "seq", split_axis=1, concat_axis=2, tiled=True)[0]
    projected = jnp.dot(
        attended,
        lax.all_gather(out_proj, "seq", axis=0, tiled=True),
        preferred_element_type=jnp.float32,
    )
    hidden = (residual_in[0].astype(jnp.float32) + projected).astype(jnp.bfloat16)
    wide = hidden.astype(jnp.float32)
    normed = (
        wide
        * lax.rsqrt(jnp.mean(wide * wide, axis=1, keepdims=True) + 1e-06)
        * norm_gain.astype(jnp.float32)
    ).astype(jnp.bfloat16)
    topk = expert_ids.shape[2]
    experts = n_seq * n_sub
    cap = max(2, (5 * tokens * topk + 4 * experts - 1) // (4 * experts))
    flat_ids = expert_ids[0].reshape(-1)
    items = flat_ids.shape[0]
    ranks = rank_in_expert(flat_ids, experts)
    slot_of = flat_ids * cap + ranks
    slots_out = experts * cap
    item_of_slot = (
        jnp.full((slots_out,), items, jnp.int32).at[slot_of].set(jnp.arange(items, dtype=jnp.int32))
    )
    padded_rows = jnp.concatenate([normed, jnp.zeros((1, D), jnp.bfloat16)], axis=0)
    padded_gates = jnp.concatenate(
        [gate_weights[0].reshape(-1), jnp.zeros((1,), jnp.bfloat16)], axis=0
    )
    token_of_slot = jnp.where(item_of_slot < items, item_of_slot // topk, tokens)
    send_rows = padded_rows[token_of_slot].reshape(experts, cap, D)
    send_gates = padded_gates[item_of_slot].reshape(experts, cap)
    recv_rows, recv_gates = (
        lax.all_to_all(send_rows, ("seq", "sub"), split_axis=0, concat_axis=0, tiled=True),
        lax.all_to_all(send_gates, ("seq", "sub"), split_axis=0, concat_axis=0, tiled=True),
    )
    slots_in = experts * cap
    valid = recv_gates > 0
    counts = jnp.sum(valid.astype(jnp.int32), axis=1)
    offsets = jnp.cumsum(counts) - counts
    dest = jnp.where(
        valid, offsets[:, None] + jnp.arange(cap, dtype=jnp.int32)[None, :], slots_in
    ).reshape(-1)
    source_of = (
        jnp.full((slots_in + 1,), slots_in, jnp.int32)
        .at[dest]
        .set(jnp.arange(slots_in, dtype=jnp.int32))[:slots_in]
    )
    compact_rows = jnp.concatenate(
        [recv_rows.reshape(slots_in, D), jnp.zeros((1, D), jnp.bfloat16)], axis=0
    )[source_of]
    compact_gates = jnp.concatenate(
        [recv_gates.reshape(-1), jnp.zeros((1,), jnp.bfloat16)], axis=0
    )[source_of].astype(jnp.float32)
    filled = jnp.sum(counts)
    n_blocks = (filled + slots_in - 1) // slots_in
    w_gate = expert_gate[0]
    w_up = expert_up[0]
    w_down = expert_down[0]

    def expert_block(index, results):
        gate_proj = jnp.dot(compact_rows, w_gate, preferred_element_type=jnp.float32)
        up_proj = jnp.dot(compact_rows, w_up, preferred_element_type=jnp.float32)
        inner = (jax.nn.silu(gate_proj) * up_proj).astype(jnp.bfloat16)
        weighted = (
            jnp.dot(inner, w_down, preferred_element_type=jnp.float32) * compact_gates[:, None]
        )
        return weighted.astype(jnp.bfloat16)

    results = lax.fori_loop(0, n_blocks, expert_block, jnp.zeros((slots_in, D), jnp.bfloat16))
    returned = jnp.concatenate([results, jnp.zeros((1, D), jnp.bfloat16)], axis=0)[dest].reshape(
        experts, cap, D
    )
    back = lax.all_to_all(
        returned, ("seq", "sub"), split_axis=0, concat_axis=0, tiled=True
    ).reshape(slots_out, D)
    gathered = back[slot_of].reshape(tokens, topk, D).astype(jnp.float32)
    mixture = jnp.sum(gathered, axis=1)
    return (wide + mixture).astype(jnp.bfloat16)[None]


PLAN = [
    [
        ("C", 0, 0), ("T", 1, 0), ("Y", 0, 0), ("T", 1, 1), ("Y", 0, 1), ("R", 0, 0),
        ("C", 1, 0), ("C", 0, 1), ("T", 2, 0), ("Y", 1, 0), ("A", 1, 0), ("A", 1, 2),
        ("T", 2, 1), ("C", 2, 0), ("Y", 2, 0), ("T", 3, 0), ("A", 2, 0), ("Y", 2, 1),
        ("A", 2, 1), ("C", 2, 1), ("T", 3, 1), ("A", 2, 2), ("C", 3, 0), ("Y", 3, 0),
        ("M", 2, 0), ("Y", 1, 1), ("S", 2, 3), ("C", 1, 1), ("Y", 3, 1), ("M", 2, 1),
        ("S", 0, 0), ("C", 3, 1), ("M", 2, 2), ("S", 1, 1), ("A", 2, 3), ("S", 3, 0),
        ("M", 1, 0), ("S", 3, 1), ("A", 3, 0), ("S", 3, 2), ("A", 3, 1), ("S", 3, 3),
        ("A", 3, 2), ("S", 1, 3), ("A", 3, 3), ("S", 0, 1), ("M", 1, 2), ("S", 0, 2),
        ("A", 0, 0), ("A", 1, 1), ("S", 0, 3), ("A", 0, 1), ("A", 1, 3), ("A", 0, 2),
        ("A", 0, 3),
    ],
    [
        ("C", 1, 0), ("T", 0, 0), ("T", 2, 0), ("Y", 1, 0), ("T", 0, 1), ("T", 2, 1),
        ("Y", 1, 1), ("C", 0, 0), ("C", 1, 1), ("T", 3, 0), ("Y", 0, 0), ("Y", 0, 1),
        ("C", 2, 0), ("C", 0, 1), ("T", 3, 1), ("Y", 2, 0), ("R", 0, 0), ("C", 3, 0),
        ("Y", 2, 1), ("C", 2, 1), ("M", 2, 3), ("Y", 3, 0), ("A", 2, 1), ("M", 0, 2),
        ("S", 0, 0), ("A", 2, 2), ("Y", 3, 1), ("S", 0, 1), ("C", 3, 1), ("S", 2, 0),
        ("M", 3, 3), ("S", 3, 0), ("M", 2, 1), ("S", 3, 1), ("A", 2, 0), ("S", 3, 2),
        ("M", 2, 2), ("S", 0, 3), ("A", 2, 3), ("S", 1, 0), ("A", 3, 0), ("S", 1, 1),
        ("A", 1, 0), ("A", 3, 1), ("S", 1, 3), ("A", 0, 0), ("A", 3, 2), ("A", 0, 1),
        ("A", 3, 3), ("A", 0, 2), ("S", 1, 2), ("A", 0, 3), ("A", 1, 1), ("A", 1, 2),
        ("A", 1, 3),
    ],
]
CODES = "TYRCSMA"


def encode_plan():
    n = len(PLAN)
    moved = [{(p, q) for what, p, q in steps if what == "M"} for steps in PLAN]
    table = []
    for here, steps in enumerate(PLAN):
        met, row = set(), []
        for what, p, q in steps:
            first = one = two = 0
            if what in "SMA":
                key = (what == "A", p)
                first = int(key not in met)
                met.add(key)
            if what == "A":
                one = int((p, q) not in moved[here])
            elif what in "SM":
                one = int(here == 1 and p >= 1 and (p, q) in moved[0])
                if here == 1:
                    two = int(p <= 1 and (3 - p, q) in moved[1])
                else:
                    two = int(p == 0 and (p, q) in moved[1])
            code = CODES.index(what)
            row.append((((((code * 4 + p) * 4 + q) * 2 + first) * 2) + one) * 2 + two)
        table.append(row)
    assert n == 2 and len(table[0]) == len(table[1])
    return table


def fetch(table, first_row, k):
    word = 0
    for w in range(0, len(table[0]), 3):
        pair = [sum(v * 1024**i for i, v in enumerate(row[w : w + 3])) for row in table]
        word = jnp.where(k // 3 == w // 3, jnp.where(first_row, pair[0], pair[1]), word)
    third = k % 3
    word = jnp.where(third == 0, word, jnp.where(third == 1, word // 1024, word // 1024**2))
    return word % 1024


def layer_kernel(
    n_sub,
    q_hbm,
    k_hbm,
    v_hbm,
    residual_hbm,
    proj_hbm,
    gain_ref,
    ids_ref,
    gates_ref,
    wg_hbm,
    wu_hbm,
    wd_hbm,
    o_ref,
    q_all,
    k_all,
    v_all,
    proj,
    residual,
    partial,
    core_far,
    core_near,
    across_near,
    wide_ref,
    q_send,
    q_recv,
    kv_send,
    kv_recv,
    part_send,
    part_recv,
    coef,
    coef_send,
    coef_recv,
    coef_up,
    coef_down,
    coef_z,
    rows,
    outs,
    from_core,
    from_y,
    from_line,
    from_moved,
    wg,
    wu,
    wd,
    load_sem,
    row_recv,
    up_send,
    down_send,
    y_send,
    core_send,
    relay_send,
    core_recv,
    result_send,
    y_recv,
    result_y_send,
    line_recv,
    line_send,
    moved_recv,
    moved_send,
    mate_send,
):
    seq = lax.axis_index("seq")
    z = lax.axis_index("sub")
    y = seq // 2
    c = seq % 2
    tokens = residual.shape[0]
    share = q_all.shape[1]
    heads = share // HD
    length = q_all.shape[0]
    group = QH // KVH
    half = tokens // 2
    me = seq * n_sub + z
    tile = coef.shape[0] // (4 * n_sub)
    quarter = tokens // 4
    plan = encode_plan()
    high = {"sub": z + 1}
    low = {"sub": z - 1}
    across = {"seq": (1 - y) * 2 + c}
    partner = {"seq": y * 2 + 1 - c}
    diagonal = {"seq": (1 - y) * 2 + 1 - c}
    mate = z + 1 - 2 * (z % 2)
    beside = {"sub": mate}
    has_high = z < n_sub - 1
    has_low = z > 0
    corner = jnp.logical_not(jnp.logical_and(has_low, has_high))
    mirrored = jnp.where(z >= n_sub // 2, 1, 0)

    def slot(yy, p, cc):
        return (yy * n_sub + p) * 2 + cc

    def piece(ref, index, h):
        return ref.at[pl.ds(pl.multiple_of(index * tokens + h * half, half), half), :]

    def remote(src, dst, send, recv, target):
        return pltpu.make_async_remote_copy(
            src_ref=src,
            dst_ref=dst,
            send_sem=send,
            recv_sem=recv,
            device_id=target,
            device_id_type=pl.DeviceIdType.MESH,
        )

    def guarded(condition, action):
        if condition is None:
            action()
        else:
            pl.when(condition)(action)

    def query_part(s):
        return q_hbm.at[:, pl.ds(pl.multiple_of(s * share, share), share)]

    def cache_part(ref, s):
        return ref.at[:, pl.ds(pl.multiple_of(s * heads // group * HD, HD), HD)]

    def token_rows(ref, s):
        return ref.at[pl.ds(pl.multiple_of(s * tokens, tokens), tokens), :]

    barrier = pltpu.get_barrier_semaphore()
    for peer in (across, partner, diagonal):
        pl.semaphore_signal(barrier, 1, device_id=peer, device_id_type=pl.DeviceIdType.MESH)

    @pl.when(has_high)
    def _():
        pl.semaphore_signal(barrier, 1, device_id=high, device_id_type=pl.DeviceIdType.MESH)

    @pl.when(has_low)
    def _():
        pl.semaphore_signal(barrier, 1, device_id=low, device_id_type=pl.DeviceIdType.MESH)

    own_parts = [
        pltpu.make_async_copy(query_part(seq), token_rows(q_all, seq), load_sem.at[0]),
        pltpu.make_async_copy(cache_part(k_hbm, seq), token_rows(k_all, seq), load_sem.at[1]),
        pltpu.make_async_copy(cache_part(v_hbm, seq), token_rows(v_all, seq), load_sem.at[2]),
        pltpu.make_async_copy(proj_hbm, proj, load_sem.at[3]),
    ]
    loads = [
        pltpu.make_async_copy(residual_hbm, residual, load_sem.at[7]),
        pltpu.make_async_copy(wg_hbm, wg, load_sem.at[4]),
        pltpu.make_async_copy(wu_hbm, wu, load_sem.at[5]),
        pltpu.make_async_copy(wd_hbm, wd, load_sem.at[6]),
    ]
    for load in own_parts + loads:
        load.start()

    lanes = 128 * ((4 * n_sub + 127) // 128)
    lane = lax.broadcasted_iota(jnp.int32, (tokens, lanes), 1)
    ids = ids_ref[...]
    gates = gates_ref[...].astype(jnp.float32)
    weights_here = jnp.zeros((tokens, lanes), jnp.float32)
    for k in range(ids.shape[1]):
        weights_here = weights_here + jnp.where(ids[:, k : k + 1] == lane, gates[:, k : k + 1], 0.0)
    identity = (
        lax.broadcasted_iota(jnp.int32, (tokens, tokens), 0)
        == lax.broadcasted_iota(jnp.int32, (tokens, tokens), 1)
    ).astype(jnp.float32).astype(jnp.bfloat16)
    turned = lax.dot_general(
        weights_here.astype(jnp.bfloat16),
        identity,
        (((0,), (0,)), ((), ())),
        preferred_element_type=jnp.float32,
    )

    def coef_tile(p, s, count=1):
        return pl.ds(pl.multiple_of((p * 4 + s) * tile, tile), count * tile)

    coef[coef_tile(z, seq), :] = turned[:tile].astype(jnp.bfloat16)

    peers = 3 + jnp.where(has_high, 1, 0) + jnp.where(has_low, 1, 0)
    with jax.named_scope("BAR"):
        pl.semaphore_wait(barrier, peers)

    others = (
        ((1 - y) * 2 + c, across),
        ((1 - y) * 2 + 1 - c, diagonal),
        (y * 2 + 1 - c, partner),
    )

    def scatter_copies(s, target):
        return (
            remote(
                cache_part(k_hbm, s),
                token_rows(k_all, seq),
                kv_send.at[s],
                kv_recv.at[seq],
                target,
            ),
            remote(
                cache_part(v_hbm, s),
                token_rows(v_all, seq),
                kv_send.at[4 + s],
                kv_recv.at[4 + seq],
                target,
            ),
            remote(
                query_part(s), token_rows(q_all, seq), q_send.at[s], q_recv.at[seq], target
            ),
        )

    def coef_near(s, target):
        here = coef.at[coef_tile(z, seq), :]
        return remote(here, here, coef_send.at[s], coef_recv.at[seq], target)

    for s, target in others:
        coef_near(s, target).start()
    for s, target in others:
        for copy in scatter_copies(s, target):
            copy.start()

    def arrival(ref, s, sem):
        return remote(token_rows(ref, s), token_rows(ref, s), q_send.at[s], sem, partner)

    def coef_hop(p, send, target):
        here = coef.at[coef_tile(p, 0, 4), :]
        return remote(here, here, send.at[p], coef_z.at[p], target)

    def coef_take(p, way):
        coef_hop(p, coef_up, high).wait_recv()

        @pl.when(has_high if way > 0 else has_low)
        def _():
            (coef_hop(p, coef_up, high) if way > 0 else coef_hop(p, coef_down, low)).start()

    def coef_step(d):
        pl.when(z - d >= 0)(lambda: coef_take(z - d, 1))
        pl.when(z + d < n_sub)(lambda: coef_take(z + d, -1))

    for load in own_parts:
        load.wait()
    with jax.named_scope("ARR"):
        for s, _ in others:
            arrival(k_all, s, kv_recv.at[s]).wait_recv()
            arrival(v_all, s, kv_recv.at[4 + s]).wait_recv()
            arrival(q_all, s, q_recv.at[s]).wait_recv()

    for s, target in others:
        there = coef.at[coef_tile(z, s), :]
        remote(there, there, coef_send.at[s], coef_recv.at[s], target).wait_recv()
    pl.when(has_high)(lambda: coef_hop(z, coef_up, high).start())
    pl.when(has_low)(lambda: coef_hop(z, coef_down, low).start())

    far_copy = remote(
        token_rows(partial, (1 - y) * 2 + 1 - c), core_far, part_send.at[0], part_recv.at[0], partner
    )
    across_copy = remote(
        token_rows(partial, (1 - y) * 2 + c),
        across_near,
        part_send.at[1],
        part_recv.at[1],
        across,
    )
    near_copy = remote(
        token_rows(partial, y * 2 + 1 - c), core_near, part_send.at[2], part_recv.at[2], partner
    )

    def attend_step(j, carry):
        yy = jnp.where(j < 2, 1 - y, y)
        cc = jnp.where(j % 2 == 0, 1 - c, c)
        i = yy * 2 + cc
        at = pl.ds(pl.multiple_of(i * tokens, tokens), tokens)
        row_pos = i * tokens + lax.broadcasted_iota(jnp.int32, (tokens, length), 0)
        col_pos = lax.broadcasted_iota(jnp.int32, (tokens, length), 1)
        allowed = row_pos >= col_pos
        outputs = []
        for head in range(heads):
            scores = lax.dot_general(
                q_all[at, head * HD : (head + 1) * HD],
                k_all[...],
                (((1,), (1,)), ((), ())),
                preferred_element_type=jnp.float32,
            ) * (1.0 / HD**0.5)
            scores = jnp.where(allowed, scores, -1e30)
            weights = jnp.exp(scores - jnp.max(scores, axis=1, keepdims=True))
            total = jnp.sum(weights, axis=1, keepdims=True)
            probs = (weights * (1.0 / total)).astype(jnp.bfloat16)
            outputs.append(
                jnp.dot(probs, v_all[...], preferred_element_type=jnp.float32).astype(jnp.bfloat16)
            )
        projected = jnp.dot(
            jnp.concatenate(outputs, axis=1), proj[...], preferred_element_type=jnp.float32
        )

        @pl.when(j != 1)
        def _():
            partial[at, :] = projected.astype(jnp.bfloat16)

        @pl.when(j == 0)
        def _():
            far_copy.start()

        @pl.when(j == 1)
        def _():
            far_copy.wait_recv()
            partial[at, :] = (projected + core_far[...].astype(jnp.float32)).astype(jnp.bfloat16)
            across_copy.start()

        @pl.when(j == 2)
        def _():
            near_copy.start()

        return carry

    with jax.named_scope("ATT"):
        lax.fori_loop(0, 4, attend_step, 0)
    coef_step(1)
    for load in loads:
        load.wait()
    coef_step(2)
    near_copy.wait_recv()
    own_rows = pl.ds(pl.multiple_of(seq * tokens, tokens), tokens)
    base = (
        residual[...].astype(jnp.float32)
        + partial[own_rows, :].astype(jnp.float32)
        + core_near[...].astype(jnp.float32)
    )
    with jax.named_scope("ACR"):
        across_copy.wait_recv()
    hidden = (base + across_near[...].astype(jnp.float32)).astype(jnp.bfloat16)
    wide_ref[...] = hidden
    wide = hidden.astype(jnp.float32)
    normed = (
        wide
        * lax.rsqrt(jnp.mean(wide * wide, axis=1, keepdims=True) + 1e-06)
        * gain_ref[...].astype(jnp.float32)[None, :]
    ).astype(jnp.bfloat16)
    own_slot = pl.ds(pl.multiple_of(slot(y, z, c) * tokens, tokens), tokens)
    rows[own_slot, :] = normed

    def row_copy(index, h, send, target):
        here = piece(rows, index, h)
        return remote(here, here, send, row_recv.at[index * 2 + h], target)

    def wait_rows(index, h):
        row_copy(index, h, relay_send.at[0], partner).wait_recv()

    def column_copies(p, h):
        index = slot(y, p, c)
        at = p * 2 + h
        return (
            (jnp.logical_and(p <= z, has_high), row_copy(index, h, up_send.at[at], high)),
            (jnp.logical_and(p >= z, has_low), row_copy(index, h, down_send.at[at], low)),
            (
                jnp.logical_or(p != mate, h == 0),
                row_copy(index, h, y_send.at[at], across),
            ),
            (None, row_copy(index, h, core_send.at[at], partner)),
        )

    def spread(p, h):
        for condition, copy in column_copies(p, h):
            guarded(condition, copy.start)

    def relay_copy(p, h):
        return row_copy(slot(1 - y, p, c), h, relay_send.at[p * 2 + h], partner)

    def result_copy(yy, p):
        index = slot(yy, p, 1 - c)
        pair = yy * n_sub + p
        src = outs.at[pl.ds(pl.multiple_of(index * tokens, tokens), tokens), :]
        dst = from_core.at[pl.ds(pl.multiple_of(pair * tokens, tokens), tokens), :]
        return remote(src, dst, result_send.at[pair], core_recv.at[pair], partner)

    mine = (
        lax.broadcasted_iota(jnp.int32, (2 * tile, 128), 0) % tile == me
    ).astype(jnp.float32).astype(jnp.bfloat16)

    def compute(yy, p):
        wait_rows(slot(yy, p, 1 - c), 0)
        wait_rows(slot(yy, p, 1 - c), 1)
        with jax.named_scope("C"):
            at = pl.ds(pl.multiple_of((yy * n_sub + p) * 2 * tokens, 2 * tokens), 2 * tokens)
            x = rows[at, :]
            gains = [
                lax.dot_general(
                    coef[coef_tile(p, 2 * yy + cc), :],
                    mine[:tile],
                    (((0,), (0,)), ((), ())),
                    preferred_element_type=jnp.float32,
                )
                for cc in range(2)
            ]
            coeff = jnp.concatenate(gains, axis=0)[:, :1]
            gate = jnp.dot(x, wg[...], preferred_element_type=jnp.float32)
            up = jnp.dot(x, wu[...], preferred_element_type=jnp.float32)
            inner = (gate / (1.0 + jnp.exp(-gate)) * up).astype(jnp.bfloat16)
            out = jnp.dot(inner, wd[...], preferred_element_type=jnp.float32)
            outs[at, :] = (out * coeff).astype(jnp.bfloat16)
        result_copy(yy, p).start()

    def mate_rows():
        return row_copy(slot(1 - y, z, c), 1, mate_send.at[0], beside)

    spread(z, 0)
    spread(z, 1)
    coef_step(3)

    def part(index, q):
        return pl.ds(pl.multiple_of(index * tokens + q * quarter, quarter), quarter)

    def y_copy(p, q):
        at = p * 4 + q
        return remote(
            outs.at[part(slot(1 - y, p, c), q), :],
            from_y.at[part(p, q), :],
            result_y_send.at[at],
            y_recv.at[at],
            across,
        )

    def passed(yy, p, q, way, buffer, send, recv):
        at = p * 4 + q
        return remote(
            outs.at[part(slot(yy, p, c), q), :],
            buffer.at[part(way * n_sub + p, q), :],
            send.at[at],
            recv.at[way * 4 * n_sub + at],
            {"sub": z + 1 - 2 * way},
        )

    def line_copy(p, q, way):
        return passed(y, p, q, way, from_line, line_send, line_recv)

    def moved_copy(p, q, way):
        return passed(1 - y, p, q, way, from_moved, moved_send, moved_recv)

    def add_to(index, q, ref, at, q_at):
        here = part(index, q)
        total = outs[here, :].astype(jnp.float32) + ref[part(at, q_at), :].astype(jnp.float32)
        outs[here, :] = total.astype(jnp.bfloat16)

    def toward(p):
        return jnp.where(p > z, 0, 1)

    def act(k, carry):
        entry = fetch(plan, corner, k)
        what = entry // 128
        place = entry // 32 % 4
        q = entry // 8 % 4
        first = entry // 4 % 2
        one = entry // 2 % 2
        two = entry % 2
        p = jnp.where(mirrored == 1, n_sub - 1 - place, place)

        @pl.when(what == CODES.index("T"))
        def _():
            wait_rows(slot(y, p, c), q)
            spread(p, q)

        @pl.when(what == CODES.index("Y"))
        def _():
            wait_rows(slot(1 - y, p, c), q)
            relay_copy(p, q).start()

        @pl.when(what == CODES.index("R"))
        def _():
            mate_rows().start()

        @pl.when(what == CODES.index("C"))
        def _():
            compute(jnp.where(q == 1, 1 - y, y), p)

        @pl.when(jnp.logical_or(what == CODES.index("S"), what == CODES.index("M")))
        def _():
            index = slot(1 - y, p, c)
            pl.when(first == 1)(lambda: result_copy(1 - y, p).wait_recv())
            add_to(index, q, from_core, (1 - y) * n_sub + p, q)

            @pl.when(one == 1)
            def _():
                moved_copy(p, q, mirrored).wait_recv()
                add_to(index, q, from_moved, mirrored * n_sub + p, q)

            @pl.when(two == 1)
            def _():
                moved_copy(p, q, 1 - mirrored).wait_recv()
                add_to(index, q, from_moved, (1 - mirrored) * n_sub + p, q)

            pl.when(what == CODES.index("S"))(lambda: y_copy(p, q).start())
            pl.when(what == CODES.index("M"))(lambda: moved_copy(p, q, toward(p)).start())

        @pl.when(what == CODES.index("A"))
        def _():
            index = slot(y, p, c)
            pl.when(first == 1)(lambda: result_copy(y, p).wait_recv())
            add_to(index, q, from_core, y * n_sub + p, q)

            @pl.when(one == 1)
            def _():
                y_copy(p, q).wait_recv()
                add_to(index, q, from_y, p, q)

            for way, comes in ((0, p >= z), (1, p <= z)):

                @pl.when(jnp.logical_and(comes, has_low if way == 0 else has_high))
                def _():
                    line_copy(p, q, way).wait_recv()
                    add_to(index, q, from_line, way * n_sub + p, q)

            pl.when(p != z)(lambda: line_copy(p, q, toward(p)).start())

            @pl.when(p == z)
            def _():
                at = part(0, q)
                o_ref[at, :] = (
                    wide_ref[at, :].astype(jnp.float32) + outs[part(index, q), :].astype(jnp.float32)
                ).astype(jnp.bfloat16)

        return carry

    with jax.named_scope("PLAN"):
        lax.fori_loop(0, len(plan[0]), act, 0)

    def drain(k, carry):
        p = k // 2
        h = k % 2
        for condition, copy in column_copies(p, h):
            guarded(condition, copy.wait_send)

        relay_copy(p, h).wait_send()
        result_copy(h, p).wait_send()

        @pl.when(h == 0)
        def _():
            pl.when(jnp.logical_and(p <= z, has_high))(lambda: coef_hop(p, coef_up, high).wait_send())
            pl.when(jnp.logical_and(p >= z, has_low))(lambda: coef_hop(p, coef_down, low).wait_send())

        return carry

    lax.fori_loop(0, 2 * n_sub, drain, 0)
    for here, steps in enumerate(PLAN):

        @pl.when(corner == (here == 0))
        def _():
            for what, place, q in steps:
                p = jnp.where(mirrored == 1, n_sub - 1 - place, place)
                if what == "S":
                    y_copy(p, q).wait_send()
                elif what == "M":
                    moved_copy(p, q, toward(p)).wait_send()
                elif what == "A" and place != here:
                    line_copy(p, q, toward(p)).wait_send()

    for s, target in others:
        for copy in scatter_copies(s, target):
            copy.wait_send()
        coef_near(s, target).wait_send()
    mate_rows().wait_send()
    far_copy.wait_send()
    across_copy.wait_send()
    near_copy.wait_send()


def layer(queries, keys, values, residual, proj, gain, ids, gates, w_gate, w_up, w_down, n_sub):
    tokens, width = residual.shape
    share = proj.shape[0]
    blocks = 4 * n_sub
    tile = 16 * ((blocks + 15) // 16)
    dma = lambda count: pltpu.SemaphoreType.DMA((count,))
    hbm = pl.BlockSpec(memory_space=pl.ANY)
    vmem = pl.BlockSpec(memory_space=pltpu.VMEM)
    bf = jnp.bfloat16
    return pl.pallas_call(
        functools.partial(layer_kernel, n_sub),
        in_specs=[hbm, hbm, hbm, hbm, hbm, vmem, vmem, vmem, hbm, hbm, hbm],
        out_specs=vmem,
        out_shape=jax.ShapeDtypeStruct((tokens, width), bf),
        scratch_shapes=[
            pltpu.VMEM((4 * tokens, share), bf),
            pltpu.VMEM((4 * tokens, HD), bf),
            pltpu.VMEM((4 * tokens, HD), bf),
            pltpu.VMEM(proj.shape, bf),
            pltpu.VMEM((tokens, width), bf),
            pltpu.VMEM((4 * tokens, width), bf),
            pltpu.VMEM((tokens, width), bf),
            pltpu.VMEM((tokens, width), bf),
            pltpu.VMEM((tokens, width), bf),
            pltpu.VMEM((tokens, width), bf),
            dma(4),
            dma(4),
            dma(8),
            dma(8),
            dma(3),
            dma(3),
            pltpu.VMEM((blocks * tile, tokens), bf),
            dma(4),
            dma(4),
            dma(n_sub),
            dma(n_sub),
            dma(n_sub),
            pltpu.VMEM((blocks * tokens, width), bf),
            pltpu.VMEM((blocks * tokens, width), bf),
            pltpu.VMEM((2 * n_sub * tokens, width), bf),
            pltpu.VMEM((n_sub * tokens, width), bf),
            pltpu.VMEM((2 * n_sub * tokens, width), bf),
            pltpu.VMEM((2 * n_sub * tokens, width), bf),
            pltpu.VMEM(w_gate.shape, bf),
            pltpu.VMEM(w_up.shape, bf),
            pltpu.VMEM(w_down.shape, bf),
            dma(8),
            dma(2 * blocks),
            dma(2 * n_sub),
            dma(2 * n_sub),
            dma(2 * n_sub),
            dma(2 * n_sub),
            dma(2 * n_sub),
            dma(2 * n_sub),
            dma(2 * n_sub),
            dma(4 * n_sub),
            dma(4 * n_sub),
            dma(8 * n_sub),
            dma(4 * n_sub),
            dma(8 * n_sub),
            dma(4 * n_sub),
            dma(1),
        ],
        compiler_params=pltpu.CompilerParams(
            collective_id=0, has_side_effects=True, vmem_limit_bytes=60 * 2**20
        ),
        name="layer",
    )(queries, keys, values, residual, proj, gain, ids, gates, w_gate, w_up, w_down)


def per_device_dense(
    query_rows,
    key_rows,
    value_rows,
    residual_in,
    out_proj,
    norm_gain,
    expert_ids,
    gate_weights,
    expert_gate,
    expert_up,
    expert_down,
):
    return layer(
        query_rows[0],
        key_rows[0],
        value_rows[0],
        residual_in[0],
        out_proj,
        norm_gain,
        expert_ids[0],
        gate_weights[0],
        expert_gate[0],
        expert_up[0],
        expert_down[0],
        lax.axis_size("sub"),
    )[None]


def per_device(*args):
    tokens = args[0].shape[1]
    topk = args[6].shape[2]
    n_seq = lax.axis_size("seq")
    experts = n_seq * lax.axis_size("sub")
    cap = max(2, (5 * tokens * topk + 4 * experts - 1) // (4 * experts))
    if 2 * cap >= tokens and n_seq == 4 and lax.axis_size("sub") == 4 and tokens == 128:
        return per_device_dense(*args)
    return per_device_routed(*args)


def solution(mesh):
    placed = (
        P(("grp", "sub"), "seq", None),
        P(("grp", "sub"), "seq", None),
        P(("grp", "sub"), "seq", None),
        P(("grp", "sub"), "seq", None),
        P("seq", None),
        P(),
        P(("grp", "sub"), "seq", None),
        P(("grp", "sub"), "seq", None),
        P(("seq", "sub"), None, None),
        P(("seq", "sub"), None, None),
        P(("seq", "sub"), None, None),
    )
    return jax.shard_map(
        per_device,
        mesh=mesh,
        in_specs=placed,
        out_specs=P(("grp", "sub"), "seq", None),
        check_vma=False,
    )
```

```python
import functools
import math
import jax
import jax.numpy as jnp
from jax import lax
from jax.experimental import pallas as pl
from jax.experimental.pallas import tpu as pltpu
from jax.sharding import PartitionSpec as P

D = 2048
HD = 128
QH = 16
KVH = 2


def attend_head(queries, keys_one, values_one, block):
    length = queries.shape[0]
    scale = 1.0 / queries.shape[1] ** 0.5
    pieces = []
    for part_index in range(length // block):
        stop = (part_index + 1) * block
        rows_here = queries[part_index * block : stop]
        scores = (
            jnp.einsum("qd,kd->qk", rows_here, keys_one[:stop], preferred_element_type=jnp.float32)
            * scale
        )
        row_pos = part_index * block + jnp.arange(block, dtype=jnp.int32)
        col_pos = jnp.arange(stop, dtype=jnp.int32)
        scores = jnp.where(row_pos[:, None] >= col_pos[None, :], scores, -1e30)
        peak = jnp.max(scores, axis=1, keepdims=True)
        weights = jnp.exp(scores - peak)
        probs = (weights / jnp.sum(weights, axis=1, keepdims=True)).astype(jnp.bfloat16)
        pieces.append(
            jnp.dot(probs, values_one[:stop], preferred_element_type=jnp.float32).astype(
                jnp.bfloat16
            )
        )
    return jnp.concatenate(pieces, axis=0)


def rank_in_expert(flat_ids, experts):
    items = flat_ids.shape[0]
    width = 128
    n_parts = items // width
    onehot = (
        (flat_ids[:, None] == jnp.arange(experts, dtype=jnp.int32)[None, :])
        .astype(jnp.bfloat16)
        .reshape(n_parts, width, experts)
    )
    lower = (
        jnp.arange(width, dtype=jnp.int32)[:, None] > jnp.arange(width, dtype=jnp.int32)[None, :]
    ).astype(jnp.bfloat16)
    within = jnp.einsum("ij,bje->bie", lower, onehot, preferred_element_type=jnp.float32)
    part_counts = jnp.sum(onehot.astype(jnp.float32), axis=1)
    earlier = jnp.cumsum(part_counts, axis=0) - part_counts
    ranks = jnp.sum((within + earlier[:, None, :]) * onehot.astype(jnp.float32), axis=2)
    return ranks.reshape(items).astype(jnp.int32)


def per_device_routed(
    query_rows,
    key_rows,
    value_rows,
    residual_in,
    out_proj,
    norm_gain,
    expert_ids,
    gate_weights,
    expert_gate,
    expert_up,
    expert_down,
):
    tokens = query_rows.shape[1]
    n_seq = lax.axis_size("seq")
    n_sub = lax.axis_size("sub")
    heads_here = QH // n_seq
    group = QH // KVH
    query_local = lax.all_to_all(query_rows, "seq", split_axis=2, concat_axis=1, tiled=True)
    key_full, value_full = (
        lax.all_gather(key_rows, "seq", axis=1, tiled=True),
        lax.all_gather(value_rows, "seq", axis=1, tiled=True),
    )
    first_head = lax.axis_index("seq") * heads_here
    key_list = []
    value_list = []
    for head in range(heads_here):
        kv_start = (first_head + head) // group * HD
        key_list.append(lax.dynamic_slice_in_dim(key_full[0], kv_start, HD, 1))
        value_list.append(lax.dynamic_slice_in_dim(value_full[0], kv_start, HD, 1))
    length = query_local.shape[1]
    block = min(length, max(512, length // 8))
    outputs = [
        attend_head(
            query_local[0, :, head * HD : (head + 1) * HD], key_list[head], value_list[head], block
        )
        for head in range(heads_here)
    ]
    head_block = jnp.concatenate(outputs, axis=1)[None]
    attended = lax.all_to_all(head_block, "seq", split_axis=1, concat_axis=2, tiled=True)[0]
    projected = jnp.dot(
        attended,
        lax.all_gather(out_proj, "seq", axis=0, tiled=True),
        preferred_element_type=jnp.float32,
    )
    hidden = (residual_in[0].astype(jnp.float32) + projected).astype(jnp.bfloat16)
    wide = hidden.astype(jnp.float32)
    normed = (
        wide
        * lax.rsqrt(jnp.mean(wide * wide, axis=1, keepdims=True) + 1e-06)
        * norm_gain.astype(jnp.float32)
    ).astype(jnp.bfloat16)
    topk = expert_ids.shape[2]
    experts = n_seq * n_sub
    cap = max(2, (5 * tokens * topk + 4 * experts - 1) // (4 * experts))
    flat_ids = expert_ids[0].reshape(-1)
    items = flat_ids.shape[0]
    ranks = rank_in_expert(flat_ids, experts)
    slot_of = flat_ids * cap + ranks
    slots_out = experts * cap
    item_of_slot = (
        jnp.full((slots_out,), items, jnp.int32).at[slot_of].set(jnp.arange(items, dtype=jnp.int32))
    )
    padded_rows = jnp.concatenate([normed, jnp.zeros((1, D), jnp.bfloat16)], axis=0)
    padded_gates = jnp.concatenate(
        [gate_weights[0].reshape(-1), jnp.zeros((1,), jnp.bfloat16)], axis=0
    )
    token_of_slot = jnp.where(item_of_slot < items, item_of_slot // topk, tokens)
    send_rows = padded_rows[token_of_slot].reshape(experts, cap, D)
    send_gates = padded_gates[item_of_slot].reshape(experts, cap)
    recv_rows, recv_gates = (
        lax.all_to_all(send_rows, ("seq", "sub"), split_axis=0, concat_axis=0, tiled=True),
        lax.all_to_all(send_gates, ("seq", "sub"), split_axis=0, concat_axis=0, tiled=True),
    )
    slots_in = experts * cap
    valid = recv_gates > 0
    counts = jnp.sum(valid.astype(jnp.int32), axis=1)
    offsets = jnp.cumsum(counts) - counts
    dest = jnp.where(
        valid, offsets[:, None] + jnp.arange(cap, dtype=jnp.int32)[None, :], slots_in
    ).reshape(-1)
    source_of = (
        jnp.full((slots_in + 1,), slots_in, jnp.int32)
        .at[dest]
        .set(jnp.arange(slots_in, dtype=jnp.int32))[:slots_in]
    )
    compact_rows = jnp.concatenate(
        [recv_rows.reshape(slots_in, D), jnp.zeros((1, D), jnp.bfloat16)], axis=0
    )[source_of]
    compact_gates = jnp.concatenate(
        [recv_gates.reshape(-1), jnp.zeros((1,), jnp.bfloat16)], axis=0
    )[source_of].astype(jnp.float32)
    filled = jnp.sum(counts)
    n_blocks = (filled + slots_in - 1) // slots_in
    w_gate = expert_gate[0]
    w_up = expert_up[0]
    w_down = expert_down[0]

    def expert_block(index, results):
        gate_proj = jnp.dot(compact_rows, w_gate, preferred_element_type=jnp.float32)
        up_proj = jnp.dot(compact_rows, w_up, preferred_element_type=jnp.float32)
        inner = (jax.nn.silu(gate_proj) * up_proj).astype(jnp.bfloat16)
        weighted = (
            jnp.dot(inner, w_down, preferred_element_type=jnp.float32) * compact_gates[:, None]
        )
        return weighted.astype(jnp.bfloat16)

    results = lax.fori_loop(0, n_blocks, expert_block, jnp.zeros((slots_in, D), jnp.bfloat16))
    returned = jnp.concatenate([results, jnp.zeros((1, D), jnp.bfloat16)], axis=0)[dest].reshape(
        experts, cap, D
    )
    back = lax.all_to_all(
        returned, ("seq", "sub"), split_axis=0, concat_axis=0, tiled=True
    ).reshape(slots_out, D)
    gathered = back[slot_of].reshape(tokens, topk, D).astype(jnp.float32)
    mixture = jnp.sum(gathered, axis=1)
    return (wide + mixture).astype(jnp.bfloat16)[None]


PLAN = [
    [
        ("C", 0, 0), ("T", 1, 0), ("Y", 0, 0), ("T", 1, 1), ("C", 1, 0), ("Y", 0, 1),
        ("R", 0, 0), ("C", 0, 1), ("T", 2, 0), ("A", 1, 2), ("Y", 1, 0), ("A", 1, 3),
        ("T", 2, 1), ("C", 2, 0), ("Y", 2, 0), ("T", 3, 0), ("A", 2, 0), ("A", 2, 1),
        ("Y", 2, 1), ("A", 2, 2), ("C", 2, 1), ("T", 3, 1), ("A", 2, 3), ("C", 3, 0),
        ("Y", 3, 0), ("Y", 1, 1), ("M", 2, 0), ("C", 1, 1), ("Y", 3, 1), ("M", 2, 1),
        ("S", 0, 0), ("C", 3, 1), ("M", 2, 2), ("S", 1, 0), ("M", 2, 3), ("S", 3, 0),
        ("M", 1, 2), ("S", 3, 1), ("A", 3, 0), ("S", 3, 2), ("A", 3, 1), ("S", 3, 3),
        ("A", 3, 2), ("S", 1, 1), ("A", 3, 3), ("S", 0, 1), ("M", 1, 3), ("S", 0, 2),
        ("A", 0, 0), ("A", 1, 0), ("S", 0, 3), ("A", 0, 1), ("A", 1, 1), ("A", 0, 2),
        ("A", 0, 3),
    ],
    [
        ("C", 1, 0), ("T", 0, 0), ("T", 2, 0), ("Y", 1, 0), ("T", 0, 1), ("T", 2, 1),
        ("C", 0, 0), ("C", 2, 0), ("T", 3, 0), ("Y", 1, 1), ("C", 1, 1), ("Y", 0, 0),
        ("Y", 0, 1), ("T", 3, 1), ("R", 0, 0), ("C", 0, 1), ("C", 3, 0), ("Y", 2, 0),
        ("Y", 2, 1), ("A", 2, 0), ("C", 2, 1), ("M", 0, 0), ("Y", 3, 0), ("A", 2, 2),
        ("M", 0, 1), ("A", 2, 3), ("S", 1, 1), ("M", 0, 3), ("Y", 3, 1), ("M", 2, 0),
        ("C", 3, 1), ("S", 2, 1), ("M", 3, 2), ("S", 3, 0), ("M", 2, 2), ("S", 3, 1),
        ("M", 0, 2), ("A", 2, 1), ("S", 3, 3), ("M", 2, 3), ("S", 1, 0), ("A", 3, 0),
        ("S", 1, 2), ("A", 3, 1), ("A", 0, 0), ("A", 3, 2), ("A", 1, 2), ("A", 0, 1),
        ("A", 3, 3), ("A", 0, 2), ("S", 1, 3), ("A", 0, 3), ("A", 1, 0), ("A", 1, 3),
        ("A", 1, 1),
    ],
]
CODES = "TYRCSMA"


def encode_plan():
    n = len(PLAN)
    moved = [{(p, q) for what, p, q in steps if what == "M"} for steps in PLAN]
    table = []
    for here, steps in enumerate(PLAN):
        met, row = set(), []
        for what, p, q in steps:
            first = one = two = 0
            if what in "SMA":
                key = (what == "A", p)
                first = int(key not in met)
                met.add(key)
            if what == "A":
                one = int((p, q) not in moved[here])
            elif what in "SM":
                one = int(here == 1 and p >= 1 and (p, q) in moved[0])
                if here == 1:
                    two = int(p <= 1 and (3 - p, q) in moved[1])
                else:
                    two = int(p == 0 and (p, q) in moved[1])
            code = CODES.index(what)
            row.append((((((code * 4 + p) * 4 + q) * 2 + first) * 2) + one) * 2 + two)
        table.append(row)
    assert n == 2 and len(table[0]) == len(table[1])
    return table


def fetch(table, first_row, k):
    word = 0
    for w in range(0, len(table[0]), 3):
        pair = [sum(v * 1024**i for i, v in enumerate(row[w : w + 3])) for row in table]
        word = jnp.where(k // 3 == w // 3, jnp.where(first_row, pair[0], pair[1]), word)
    third = k % 3
    word = jnp.where(third == 0, word, jnp.where(third == 1, word // 1024, word // 1024**2))
    return word % 1024


def layer_kernel(
    n_sub,
    q_hbm,
    k_hbm,
    v_hbm,
    residual_hbm,
    proj_hbm,
    gain_hbm,
    ids_hbm,
    gates_hbm,
    wg_hbm,
    wu_hbm,
    wd_hbm,
    o_hbm,
    gain_ref,
    ids_ref,
    gates_ref,
    o_ref,
    o_sem,
    q_all,
    k_all,
    v_all,
    proj,
    residual,
    partial,
    core_far,
    core_near,
    across_near,
    wide_ref,
    q_send,
    q_recv,
    kv_send,
    kv_recv,
    part_send,
    part_recv,
    coef,
    coef_send,
    coef_recv,
    coef_up,
    coef_down,
    coef_z,
    rows,
    outs,
    from_core,
    from_y,
    from_line,
    from_moved,
    wg,
    wu,
    wd,
    load_sem,
    row_recv,
    up_send,
    down_send,
    y_send,
    core_send,
    relay_send,
    core_recv,
    result_send,
    y_recv,
    result_y_send,
    line_recv,
    line_send,
    moved_recv,
    moved_send,
    mate_send,
):
    seq = lax.axis_index("seq")
    z = lax.axis_index("sub")
    y = seq // 2
    c = seq % 2
    tokens = residual.shape[0]
    share = q_all.shape[1]
    heads = share // HD
    length = q_all.shape[0]
    group = QH // KVH
    half = tokens // 2
    me = seq * n_sub + z
    tile = coef.shape[0] // (4 * n_sub)
    quarter = tokens // 4
    plan = encode_plan()
    high = {"sub": z + 1}
    low = {"sub": z - 1}
    across = {"seq": (1 - y) * 2 + c}
    partner = {"seq": y * 2 + 1 - c}
    diagonal = {"seq": (1 - y) * 2 + 1 - c}
    mate = z + 1 - 2 * (z % 2)
    beside = {"sub": mate}
    has_high = z < n_sub - 1
    has_low = z > 0
    corner = jnp.logical_not(jnp.logical_and(has_low, has_high))
    mirrored = jnp.where(z >= n_sub // 2, 1, 0)

    def slot(yy, p, cc):
        return (yy * n_sub + p) * 2 + cc

    def piece(ref, index, h):
        return ref.at[pl.ds(pl.multiple_of(index * tokens + h * half, half), half), :]

    def remote(src, dst, send, recv, target):
        return pltpu.make_async_remote_copy(
            src_ref=src,
            dst_ref=dst,
            send_sem=send,
            recv_sem=recv,
            device_id=target,
            device_id_type=pl.DeviceIdType.MESH,
        )

    def guarded(condition, action):
        if condition is None:
            action()
        else:
            pl.when(condition)(action)

    def query_part(s, h):
        return q_hbm.at[pl.ds(h * half, half), pl.ds(pl.multiple_of(s * share, share), share)]

    def cache_part(ref, s):
        return ref.at[:, pl.ds(pl.multiple_of(s * heads // group * HD, HD), HD)]

    def token_rows(ref, s):
        return ref.at[pl.ds(pl.multiple_of(s * tokens, tokens), tokens), :]

    def half_rows(s, h):
        return pl.ds(pl.multiple_of(((s // 2 * 2 + h) * 2 + s % 2) * half, half), half)

    barrier = pltpu.get_barrier_semaphore()
    for peer in (across, partner, diagonal):
        pl.semaphore_signal(barrier, 1, device_id=peer, device_id_type=pl.DeviceIdType.MESH)

    @pl.when(has_high)
    def _():
        pl.semaphore_signal(barrier, 1, device_id=high, device_id_type=pl.DeviceIdType.MESH)

    @pl.when(has_low)
    def _():
        pl.semaphore_signal(barrier, 1, device_id=low, device_id_type=pl.DeviceIdType.MESH)

    small = [
        pltpu.make_async_copy(ids_hbm, ids_ref, load_sem.at[8]),
        pltpu.make_async_copy(gates_hbm, gates_ref, load_sem.at[9]),
    ]
    own_parts = [
        pltpu.make_async_copy(cache_part(k_hbm, seq), token_rows(k_all, seq), load_sem.at[1]),
        pltpu.make_async_copy(cache_part(v_hbm, seq), token_rows(v_all, seq), load_sem.at[2]),
        pltpu.make_async_copy(query_part(seq, 0), q_all.at[half_rows(seq, 0), :], load_sem.at[0]),
        pltpu.make_async_copy(query_part(seq, 1), q_all.at[half_rows(seq, 1), :], load_sem.at[11]),
        pltpu.make_async_copy(proj_hbm, proj, load_sem.at[3]),
    ]
    loads = [
        pltpu.make_async_copy(residual_hbm, residual, load_sem.at[7]),
        pltpu.make_async_copy(gain_hbm, gain_ref, load_sem.at[10]),
        pltpu.make_async_copy(wg_hbm, wg, load_sem.at[4]),
        pltpu.make_async_copy(wu_hbm, wu, load_sem.at[5]),
        pltpu.make_async_copy(wd_hbm, wd, load_sem.at[6]),
    ]
    for load in small + own_parts + loads:
        load.start()

    def coef_tile(p, s, count=1):
        return pl.ds(pl.multiple_of((p * 4 + s) * tile, tile), count * tile)

    for load in small:
        load.wait()
    expert = lax.broadcasted_iota(jnp.int32, (tile, tokens), 0)
    ids = ids_ref[...]
    gates = gates_ref[...].astype(jnp.float32)
    weights_here = jnp.zeros((tile, tokens), jnp.float32)
    for k in range(ids.shape[0]):
        weights_here = weights_here + jnp.where(ids[k : k + 1, :] == expert, gates[k : k + 1, :], 0.0)
    coef[coef_tile(z, seq), :] = weights_here.astype(jnp.bfloat16)
    peers = 3 + jnp.where(has_high, 1, 0) + jnp.where(has_low, 1, 0)
    with jax.named_scope("BAR"):
        pl.semaphore_wait(barrier, peers)

    others = (
        ((1 - y) * 2 + c, across),
        ((1 - y) * 2 + 1 - c, diagonal),
        (y * 2 + 1 - c, partner),
    )

    def cache_copies(s, target):
        return (
            remote(
                cache_part(k_hbm, s),
                token_rows(k_all, seq),
                kv_send.at[s],
                kv_recv.at[seq],
                target,
            ),
            remote(
                cache_part(v_hbm, s),
                token_rows(v_all, seq),
                kv_send.at[4 + s],
                kv_recv.at[4 + seq],
                target,
            ),
        )

    def query_copy(s, h, target):
        return remote(
            query_part(s, h),
            q_all.at[half_rows(seq, h), :],
            q_send.at[s * 2 + h],
            q_recv.at[seq * 2 + h],
            target,
        )

    def coef_near(s, target):
        here = coef.at[coef_tile(z, seq), :]
        return remote(here, here, coef_send.at[s], coef_recv.at[seq], target)

    for s, target in others:
        coef_near(s, target).start()
        for copy in cache_copies(s, target):
            copy.start()
    for h in range(2):
        for s, target in others:
            query_copy(s, h, target).start()

    def arrival(ref, s, sem):
        return remote(token_rows(ref, s), token_rows(ref, s), q_send.at[s], sem, partner)

    def coef_hop(p, send, target):
        here = coef.at[coef_tile(p, 0, 4), :]
        return remote(here, here, send.at[p], coef_z.at[p], target)

    def coef_take(p, way):
        coef_hop(p, coef_up, high).wait_recv()

        @pl.when(has_high if way > 0 else has_low)
        def _():
            (coef_hop(p, coef_up, high) if way > 0 else coef_hop(p, coef_down, low)).start()

    def coef_step(d):
        pl.when(z - d >= 0)(lambda: coef_take(z - d, 1))
        pl.when(z + d < n_sub)(lambda: coef_take(z + d, -1))

    for load in own_parts:
        load.wait()
    with jax.named_scope("ARR"):
        for s, _ in others:
            arrival(k_all, s, kv_recv.at[s]).wait_recv()
            arrival(v_all, s, kv_recv.at[4 + s]).wait_recv()

    def half_copy(src_rows, dst, h, at, target):
        return remote(
            partial.at[src_rows, :],
            dst.at[pl.ds(pl.multiple_of(h * half, half), half), :],
            part_send.at[at * 2 + h],
            part_recv.at[at * 2 + h],
            target,
        )

    def far_copy(h):
        return half_copy(half_rows((1 - y) * 2 + 1 - c, h), core_far, h, 0, partner)

    def across_copy(h):
        return half_copy(half_rows((1 - y) * 2 + c, h), across_near, h, 1, across)

    def near_copy(h):
        return half_copy(half_rows(y * 2 + 1 - c, h), core_near, h, 2, partner)

    def half_at(h):
        return pl.ds(pl.multiple_of(h * half, half), half)

    def attend_step(t, carry):
        h = t // 2
        other = jnp.logical_or(t == 1, t == 2)
        yy = jnp.where(other, 1 - y, y)
        at = pl.ds(pl.multiple_of((yy * 2 + h) * tokens, tokens), tokens)

        for cc in range(2):

            @pl.when(yy * 2 + cc != seq)
            def _():
                block = q_all.at[half_rows(yy * 2 + cc, h), :]
                arrived = q_recv.at[(yy * 2 + cc) * 2 + h]
                remote(block, block, q_send.at[0], arrived, partner).wait_recv()

        @pl.when(t == 2)
        def _():
            send_sum(0)

        with jax.named_scope("A1"):
            row = lax.broadcasted_iota(jnp.int32, (tokens, 1), 0)
            row_pos = yy * 2 * tokens + h * half + row + jnp.where(row >= half, tokens - half, 0)
            col_pos = lax.broadcasted_iota(jnp.int32, (tokens, length), 1)
            allowed = row_pos >= col_pos
            scores = lax.dot_general(
                jnp.concatenate([q_all[at, head * HD : (head + 1) * HD] for head in range(heads)], axis=0),
                k_all[...],
                (((1,), (1,)), ((), ())),
                preferred_element_type=jnp.float32,
            )
            chances, totals = [], []
            for head in range(heads):
                raw = jnp.where(allowed, scores[head * tokens : (head + 1) * tokens], -1e30)
                peak = jnp.max(raw, axis=1, keepdims=True)
                weights = jnp.exp2((raw - peak) * (math.log2(math.e) / HD**0.5))
                totals.append(jnp.sum(weights, axis=1, keepdims=True))
                chances.append(weights.astype(jnp.bfloat16))
            mixed = jnp.dot(
                jnp.concatenate(chances, axis=0), v_all[...], preferred_element_type=jnp.float32
            )
            outputs = [
                (mixed[head * tokens : (head + 1) * tokens] * (1.0 / totals[head])).astype(jnp.bfloat16)
                for head in range(heads)
            ]
        partial[at, :] = jnp.dot(
            jnp.concatenate(outputs, axis=1), proj[...], preferred_element_type=jnp.float32
        ).astype(jnp.bfloat16)

        pl.when(other)(lambda: far_copy(h).start())
        pl.when(jnp.logical_not(other))(lambda: near_copy(h).start())

        @pl.when(t == 0)
        def _():
            for s, target in others:
                there = coef.at[coef_tile(z, s), :]
                remote(there, there, coef_send.at[s], coef_recv.at[s], target).wait_recv()
            pl.when(has_high)(lambda: coef_hop(z, coef_up, high).start())
            pl.when(has_low)(lambda: coef_hop(z, coef_down, low).start())

        pl.when(t == 1)(lambda: coef_step(1))
        return carry

    def send_sum(h):
        far_copy(h).wait_recv()
        at = half_rows((1 - y) * 2 + c, h)
        total = partial[at, :].astype(jnp.float32) + core_far[half_at(h), :].astype(jnp.float32)
        partial[at, :] = total.astype(jnp.bfloat16)
        across_copy(h).start()

    with jax.named_scope("ATT"):
        lax.fori_loop(0, 4, attend_step, 0)
    send_sum(1)
    coef_step(2)
    for load in loads:
        load.wait()

    def finish(h):
        near_copy(h).wait_recv()
        with jax.named_scope("ACR"):
            across_copy(h).wait_recv()
        at = half_at(h)
        hidden = (
            residual[at, :].astype(jnp.float32)
            + partial[half_rows(seq, h), :].astype(jnp.float32)
            + core_near[at, :].astype(jnp.float32)
            + across_near[at, :].astype(jnp.float32)
        ).astype(jnp.bfloat16)
        wide_ref[at, :] = hidden
        wide = hidden.astype(jnp.float32)
        normed = (
            wide
            * lax.rsqrt(jnp.mean(wide * wide, axis=1, keepdims=True) + 1e-06)
            * gain_ref[...].astype(jnp.float32)[None, :]
        ).astype(jnp.bfloat16)
        index = slot(y, z, c)
        rows[pl.ds(pl.multiple_of(index * tokens + h * half, half), half), :] = normed
        spread(z, h)

    def row_copy(index, h, send, target):
        here = piece(rows, index, h)
        return remote(here, here, send, row_recv.at[index * 2 + h], target)

    def wait_rows(index, h):
        row_copy(index, h, relay_send.at[0], partner).wait_recv()

    def column_copies(p, h):
        index = slot(y, p, c)
        at = p * 2 + h
        return (
            (jnp.logical_and(p <= z, has_high), row_copy(index, h, up_send.at[at], high)),
            (jnp.logical_and(p >= z, has_low), row_copy(index, h, down_send.at[at], low)),
            (
                jnp.logical_or(p != mate, h == 0),
                row_copy(index, h, y_send.at[at], across),
            ),
            (None, row_copy(index, h, core_send.at[at], partner)),
        )

    def spread(p, h):
        for condition, copy in column_copies(p, h):
            guarded(condition, copy.start)

    def relay_copy(p, h):
        return row_copy(slot(1 - y, p, c), h, relay_send.at[p * 2 + h], partner)

    def result_copy(yy, p):
        index = slot(yy, p, 1 - c)
        pair = yy * n_sub + p
        src = outs.at[pl.ds(pl.multiple_of(index * tokens, tokens), tokens), :]
        dst = from_core.at[pl.ds(pl.multiple_of(pair * tokens, tokens), tokens), :]
        return remote(src, dst, result_send.at[pair], core_recv.at[pair], partner)

    mine = (
        lax.broadcasted_iota(jnp.int32, (2 * tile, 128), 0) % tile == me
    ).astype(jnp.float32).astype(jnp.bfloat16)

    def compute(yy, p):
        wait_rows(slot(yy, p, 1 - c), 0)
        wait_rows(slot(yy, p, 1 - c), 1)
        with jax.named_scope("C"):
            at = pl.ds(pl.multiple_of((yy * n_sub + p) * 2 * tokens, 2 * tokens), 2 * tokens)
            x = rows[at, :]
            gains = [
                lax.dot_general(
                    coef[coef_tile(p, 2 * yy + cc), :],
                    mine[:tile],
                    (((0,), (0,)), ((), ())),
                    preferred_element_type=jnp.float32,
                )
                for cc in range(2)
            ]
            coeff = jnp.concatenate(gains, axis=0)[:, :1]
            gate = jnp.dot(x, wg[...], preferred_element_type=jnp.float32)
            up = jnp.dot(x, wu[...], preferred_element_type=jnp.float32)
            inner = (gate / (1.0 + jnp.exp(-gate)) * up).astype(jnp.bfloat16)
            out = jnp.dot(inner, wd[...], preferred_element_type=jnp.float32)
            outs[at, :] = (out * coeff).astype(jnp.bfloat16)
        result_copy(yy, p).start()

    def mate_rows():
        return row_copy(slot(1 - y, z, c), 1, mate_send.at[0], beside)

    finish(0)
    finish(1)
    coef_step(3)

    def part(index, q):
        return pl.ds(pl.multiple_of(index * tokens + q * quarter, quarter), quarter)

    def y_copy(p, q):
        at = p * 4 + q
        return remote(
            outs.at[part(slot(1 - y, p, c), q), :],
            from_y.at[part(p, q), :],
            result_y_send.at[at],
            y_recv.at[at],
            across,
        )

    def passed(yy, p, q, way, buffer, send, recv):
        at = p * 4 + q
        return remote(
            outs.at[part(slot(yy, p, c), q), :],
            buffer.at[part(way * n_sub + p, q), :],
            send.at[at],
            recv.at[way * 4 * n_sub + at],
            {"sub": z + 1 - 2 * way},
        )

    def line_copy(p, q, way):
        return passed(y, p, q, way, from_line, line_send, line_recv)

    def moved_copy(p, q, way):
        return passed(1 - y, p, q, way, from_moved, moved_send, moved_recv)

    def add_to(index, q, ref, at, q_at):
        here = part(index, q)
        total = outs[here, :].astype(jnp.float32) + ref[part(at, q_at), :].astype(jnp.float32)
        outs[here, :] = total.astype(jnp.bfloat16)

    def out_copy(q):
        return pltpu.make_async_copy(o_ref.at[part(0, q), :], o_hbm.at[part(0, q), :], o_sem.at[q])

    def toward(p):
        return jnp.where(p > z, 0, 1)

    def act(k, carry):
        entry = fetch(plan, corner, k)
        what = entry // 128
        place = entry // 32 % 4
        q = entry // 8 % 4
        first = entry // 4 % 2
        one = entry // 2 % 2
        two = entry % 2
        p = jnp.where(mirrored == 1, n_sub - 1 - place, place)

        @pl.when(what == CODES.index("T"))
        def _():
            wait_rows(slot(y, p, c), q)
            spread(p, q)

        @pl.when(what == CODES.index("Y"))
        def _():
            wait_rows(slot(1 - y, p, c), q)
            relay_copy(p, q).start()

        @pl.when(what == CODES.index("R"))
        def _():
            mate_rows().start()

        @pl.when(what == CODES.index("C"))
        def _():
            compute(jnp.where(q == 1, 1 - y, y), p)

        @pl.when(jnp.logical_or(what == CODES.index("S"), what == CODES.index("M")))
        def _():
            index = slot(1 - y, p, c)
            pl.when(first == 1)(lambda: result_copy(1 - y, p).wait_recv())
            add_to(index, q, from_core, (1 - y) * n_sub + p, q)

            @pl.when(one == 1)
            def _():
                moved_copy(p, q, mirrored).wait_recv()
                add_to(index, q, from_moved, mirrored * n_sub + p, q)

            @pl.when(two == 1)
            def _():
                moved_copy(p, q, 1 - mirrored).wait_recv()
                add_to(index, q, from_moved, (1 - mirrored) * n_sub + p, q)

            pl.when(what == CODES.index("S"))(lambda: y_copy(p, q).start())
            pl.when(what == CODES.index("M"))(lambda: moved_copy(p, q, toward(p)).start())

        @pl.when(what == CODES.index("A"))
        def _():
            index = slot(y, p, c)
            pl.when(first == 1)(lambda: result_copy(y, p).wait_recv())
            add_to(index, q, from_core, y * n_sub + p, q)

            @pl.when(one == 1)
            def _():
                y_copy(p, q).wait_recv()
                add_to(index, q, from_y, p, q)

            for way, comes in ((0, p >= z), (1, p <= z)):

                @pl.when(jnp.logical_and(comes, has_low if way == 0 else has_high))
                def _():
                    line_copy(p, q, way).wait_recv()
                    add_to(index, q, from_line, way * n_sub + p, q)

            pl.when(p != z)(lambda: line_copy(p, q, toward(p)).start())

            @pl.when(p == z)
            def _():
                at = part(0, q)
                o_ref[at, :] = (
                    wide_ref[at, :].astype(jnp.float32) + outs[part(index, q), :].astype(jnp.float32)
                ).astype(jnp.bfloat16)
                out_copy(q).start()

        return carry

    with jax.named_scope("PLAN"):
        lax.fori_loop(0, len(plan[0]), act, 0)

    def drain(k, carry):
        p = k // 2
        h = k % 2
        for condition, copy in column_copies(p, h):
            guarded(condition, copy.wait_send)

        relay_copy(p, h).wait_send()
        result_copy(h, p).wait_send()

        @pl.when(h == 0)
        def _():
            pl.when(jnp.logical_and(p <= z, has_high))(lambda: coef_hop(p, coef_up, high).wait_send())
            pl.when(jnp.logical_and(p >= z, has_low))(lambda: coef_hop(p, coef_down, low).wait_send())

        return carry

    lax.fori_loop(0, 2 * n_sub, drain, 0)
    for here, steps in enumerate(PLAN):

        @pl.when(corner == (here == 0))
        def _():
            for what, place, q in steps:
                p = jnp.where(mirrored == 1, n_sub - 1 - place, place)
                if what == "S":
                    y_copy(p, q).wait_send()
                elif what == "M":
                    moved_copy(p, q, toward(p)).wait_send()
                elif what == "A" and place != here:
                    line_copy(p, q, toward(p)).wait_send()

    for s, target in others:
        for copy in cache_copies(s, target):
            copy.wait_send()
        coef_near(s, target).wait_send()
        for h in range(2):
            query_copy(s, h, target).wait_send()
    mate_rows().wait_send()
    for h in range(2):
        far_copy(h).wait_send()
        across_copy(h).wait_send()
        near_copy(h).wait_send()
    for q in range(4):
        out_copy(q).wait()


def layer(queries, keys, values, residual, proj, gain, ids, gates, w_gate, w_up, w_down, n_sub):
    tokens, width = residual.shape
    share = proj.shape[0]
    blocks = 4 * n_sub
    tile = 16 * ((blocks + 15) // 16)
    dma = lambda count: pltpu.SemaphoreType.DMA((count,))
    hbm = pl.BlockSpec(memory_space=pl.ANY)
    bf = jnp.bfloat16
    return pl.pallas_call(
        functools.partial(layer_kernel, n_sub),
        in_specs=[hbm] * 11,
        out_specs=hbm,
        out_shape=jax.ShapeDtypeStruct((tokens, width), bf),
        scratch_shapes=[
            pltpu.VMEM(gain.shape, bf),
            pltpu.VMEM(ids.shape, jnp.int32),
            pltpu.VMEM(gates.shape, bf),
            pltpu.VMEM((tokens, width), bf),
            dma(4),
            pltpu.VMEM((4 * tokens, share), bf),
            pltpu.VMEM((4 * tokens, HD), bf),
            pltpu.VMEM((4 * tokens, HD), bf),
            pltpu.VMEM(proj.shape, bf),
            pltpu.VMEM((tokens, width), bf),
            pltpu.VMEM((4 * tokens, width), bf),
            pltpu.VMEM((tokens, width), bf),
            pltpu.VMEM((tokens, width), bf),
            pltpu.VMEM((tokens, width), bf),
            pltpu.VMEM((tokens, width), bf),
            dma(8),
            dma(8),
            dma(8),
            dma(8),
            dma(6),
            dma(6),
            pltpu.VMEM((blocks * tile, tokens), bf),
            dma(4),
            dma(4),
            dma(n_sub),
            dma(n_sub),
            dma(n_sub),
            pltpu.VMEM((blocks * tokens, width), bf),
            pltpu.VMEM((blocks * tokens, width), bf),
            pltpu.VMEM((2 * n_sub * tokens, width), bf),
            pltpu.VMEM((n_sub * tokens, width), bf),
            pltpu.VMEM((2 * n_sub * tokens, width), bf),
            pltpu.VMEM((2 * n_sub * tokens, width), bf),
            pltpu.VMEM(w_gate.shape, bf),
            pltpu.VMEM(w_up.shape, bf),
            pltpu.VMEM(w_down.shape, bf),
            dma(12),
            dma(2 * blocks),
            dma(2 * n_sub),
            dma(2 * n_sub),
            dma(2 * n_sub),
            dma(2 * n_sub),
            dma(2 * n_sub),
            dma(2 * n_sub),
            dma(2 * n_sub),
            dma(4 * n_sub),
            dma(4 * n_sub),
            dma(8 * n_sub),
            dma(4 * n_sub),
            dma(8 * n_sub),
            dma(4 * n_sub),
            dma(1),
        ],
        compiler_params=pltpu.CompilerParams(
            collective_id=0, has_side_effects=True, vmem_limit_bytes=60 * 2**20
        ),
        name="layer",
    )(queries, keys, values, residual, proj, gain, ids, gates, w_gate, w_up, w_down)


def per_device_dense(
    query_rows,
    key_rows,
    value_rows,
    residual_in,
    out_proj,
    norm_gain,
    expert_ids,
    gate_weights,
    expert_gate,
    expert_up,
    expert_down,
):
    return layer(
        query_rows[0],
        key_rows[0],
        value_rows[0],
        residual_in[0],
        out_proj,
        norm_gain,
        expert_ids[0].T,
        gate_weights[0].T,
        expert_gate[0],
        expert_up[0],
        expert_down[0],
        lax.axis_size("sub"),
    )[None]


def per_device(*args):
    tokens = args[0].shape[1]
    topk = args[6].shape[2]
    n_seq = lax.axis_size("seq")
    experts = n_seq * lax.axis_size("sub")
    cap = max(2, (5 * tokens * topk + 4 * experts - 1) // (4 * experts))
    if 2 * cap >= tokens and n_seq == 4 and lax.axis_size("sub") == 4 and tokens == 128:
        return per_device_dense(*args)
    return per_device_routed(*args)


def solution(mesh):
    placed = (
        P(("grp", "sub"), "seq", None),
        P(("grp", "sub"), "seq", None),
        P(("grp", "sub"), "seq", None),
        P(("grp", "sub"), "seq", None),
        P("seq", None),
        P(),
        P(("grp", "sub"), "seq", None),
        P(("grp", "sub"), "seq", None),
        P(("seq", "sub"), None, None),
        P(("seq", "sub"), None, None),
        P(("seq", "sub"), None, None),
    )
    return jax.shard_map(
        per_device,
        mesh=mesh,
        in_specs=placed,
        out_specs=P(("grp", "sub"), "seq", None),
        check_vma=False,
    )
```

```python
import functools
import math
import jax
import jax.numpy as jnp
from jax import lax
from jax.experimental import pallas as pl
from jax.experimental.pallas import tpu as pltpu
from jax.sharding import PartitionSpec as P

D = 2048
HD = 128
QH = 16
KVH = 2


def attend_head(queries, keys_one, values_one, block):
    length = queries.shape[0]
    scale = 1.0 / queries.shape[1] ** 0.5
    pieces = []
    for part_index in range(length // block):
        stop = (part_index + 1) * block
        rows_here = queries[part_index * block : stop]
        scores = (
            jnp.einsum("qd,kd->qk", rows_here, keys_one[:stop], preferred_element_type=jnp.float32)
            * scale
        )
        row_pos = part_index * block + jnp.arange(block, dtype=jnp.int32)
        col_pos = jnp.arange(stop, dtype=jnp.int32)
        scores = jnp.where(row_pos[:, None] >= col_pos[None, :], scores, -1e30)
        peak = jnp.max(scores, axis=1, keepdims=True)
        weights = jnp.exp(scores - peak)
        probs = (weights / jnp.sum(weights, axis=1, keepdims=True)).astype(jnp.bfloat16)
        pieces.append(
            jnp.dot(probs, values_one[:stop], preferred_element_type=jnp.float32).astype(
                jnp.bfloat16
            )
        )
    return jnp.concatenate(pieces, axis=0)


def rank_in_expert(flat_ids, experts):
    items = flat_ids.shape[0]
    width = 128
    n_parts = items // width
    onehot = (
        (flat_ids[:, None] == jnp.arange(experts, dtype=jnp.int32)[None, :])
        .astype(jnp.bfloat16)
        .reshape(n_parts, width, experts)
    )
    lower = (
        jnp.arange(width, dtype=jnp.int32)[:, None] > jnp.arange(width, dtype=jnp.int32)[None, :]
    ).astype(jnp.bfloat16)
    within = jnp.einsum("ij,bje->bie", lower, onehot, preferred_element_type=jnp.float32)
    part_counts = jnp.sum(onehot.astype(jnp.float32), axis=1)
    earlier = jnp.cumsum(part_counts, axis=0) - part_counts
    ranks = jnp.sum((within + earlier[:, None, :]) * onehot.astype(jnp.float32), axis=2)
    return ranks.reshape(items).astype(jnp.int32)


def per_device_routed(
    query_rows,
    key_rows,
    value_rows,
    residual_in,
    out_proj,
    norm_gain,
    expert_ids,
    gate_weights,
    expert_gate,
    expert_up,
    expert_down,
):
    tokens = query_rows.shape[1]
    n_seq = lax.axis_size("seq")
    n_sub = lax.axis_size("sub")
    heads_here = QH // n_seq
    group = QH // KVH
    query_local = lax.all_to_all(query_rows, "seq", split_axis=2, concat_axis=1, tiled=True)
    key_full, value_full = (
        lax.all_gather(key_rows, "seq", axis=1, tiled=True),
        lax.all_gather(value_rows, "seq", axis=1, tiled=True),
    )
    first_head = lax.axis_index("seq") * heads_here
    key_list = []
    value_list = []
    for head in range(heads_here):
        kv_start = (first_head + head) // group * HD
        key_list.append(lax.dynamic_slice_in_dim(key_full[0], kv_start, HD, 1))
        value_list.append(lax.dynamic_slice_in_dim(value_full[0], kv_start, HD, 1))
    length = query_local.shape[1]
    block = min(length, max(512, length // 8))
    outputs = [
        attend_head(
            query_local[0, :, head * HD : (head + 1) * HD], key_list[head], value_list[head], block
        )
        for head in range(heads_here)
    ]
    head_block = jnp.concatenate(outputs, axis=1)[None]
    attended = lax.all_to_all(head_block, "seq", split_axis=1, concat_axis=2, tiled=True)[0]
    projected = jnp.dot(
        attended,
        lax.all_gather(out_proj, "seq", axis=0, tiled=True),
        preferred_element_type=jnp.float32,
    )
    hidden = (residual_in[0].astype(jnp.float32) + projected).astype(jnp.bfloat16)
    wide = hidden.astype(jnp.float32)
    normed = (
        wide
        * lax.rsqrt(jnp.mean(wide * wide, axis=1, keepdims=True) + 1e-06)
        * norm_gain.astype(jnp.float32)
    ).astype(jnp.bfloat16)
    topk = expert_ids.shape[2]
    experts = n_seq * n_sub
    cap = max(2, (5 * tokens * topk + 4 * experts - 1) // (4 * experts))
    flat_ids = expert_ids[0].reshape(-1)
    items = flat_ids.shape[0]
    ranks = rank_in_expert(flat_ids, experts)
    slot_of = flat_ids * cap + ranks
    slots_out = experts * cap
    item_of_slot = (
        jnp.full((slots_out,), items, jnp.int32).at[slot_of].set(jnp.arange(items, dtype=jnp.int32))
    )
    padded_rows = jnp.concatenate([normed, jnp.zeros((1, D), jnp.bfloat16)], axis=0)
    padded_gates = jnp.concatenate(
        [gate_weights[0].reshape(-1), jnp.zeros((1,), jnp.bfloat16)], axis=0
    )
    token_of_slot = jnp.where(item_of_slot < items, item_of_slot // topk, tokens)
    send_rows = padded_rows[token_of_slot].reshape(experts, cap, D)
    send_gates = padded_gates[item_of_slot].reshape(experts, cap)
    recv_rows, recv_gates = (
        lax.all_to_all(send_rows, ("seq", "sub"), split_axis=0, concat_axis=0, tiled=True),
        lax.all_to_all(send_gates, ("seq", "sub"), split_axis=0, concat_axis=0, tiled=True),
    )
    slots_in = experts * cap
    valid = recv_gates > 0
    counts = jnp.sum(valid.astype(jnp.int32), axis=1)
    offsets = jnp.cumsum(counts) - counts
    dest = jnp.where(
        valid, offsets[:, None] + jnp.arange(cap, dtype=jnp.int32)[None, :], slots_in
    ).reshape(-1)
    source_of = (
        jnp.full((slots_in + 1,), slots_in, jnp.int32)
        .at[dest]
        .set(jnp.arange(slots_in, dtype=jnp.int32))[:slots_in]
    )
    compact_rows = jnp.concatenate(
        [recv_rows.reshape(slots_in, D), jnp.zeros((1, D), jnp.bfloat16)], axis=0
    )[source_of]
    compact_gates = jnp.concatenate(
        [recv_gates.reshape(-1), jnp.zeros((1,), jnp.bfloat16)], axis=0
    )[source_of].astype(jnp.float32)
    filled = jnp.sum(counts)
    n_blocks = (filled + slots_in - 1) // slots_in
    w_gate = expert_gate[0]
    w_up = expert_up[0]
    w_down = expert_down[0]

    def expert_block(index, results):
        gate_proj = jnp.dot(compact_rows, w_gate, preferred_element_type=jnp.float32)
        up_proj = jnp.dot(compact_rows, w_up, preferred_element_type=jnp.float32)
        inner = (jax.nn.silu(gate_proj) * up_proj).astype(jnp.bfloat16)
        weighted = (
            jnp.dot(inner, w_down, preferred_element_type=jnp.float32) * compact_gates[:, None]
        )
        return weighted.astype(jnp.bfloat16)

    results = lax.fori_loop(0, n_blocks, expert_block, jnp.zeros((slots_in, D), jnp.bfloat16))
    returned = jnp.concatenate([results, jnp.zeros((1, D), jnp.bfloat16)], axis=0)[dest].reshape(
        experts, cap, D
    )
    back = lax.all_to_all(
        returned, ("seq", "sub"), split_axis=0, concat_axis=0, tiled=True
    ).reshape(slots_out, D)
    gathered = back[slot_of].reshape(tokens, topk, D).astype(jnp.float32)
    mixture = jnp.sum(gathered, axis=1)
    return (wide + mixture).astype(jnp.bfloat16)[None]


PLAN = [
    [
        ("C", 0, 2), ("T", 1, 0), ("C", 1, 0), ("Y", 0, 0), ("C", 0, 1), ("T", 1, 1),
        ("C", 1, 2), ("Y", 0, 1), ("R", 0, 0), ("C", 0, 3), ("T", 2, 0), ("A", 1, 0),
        ("C", 2, 0), ("Y", 1, 0), ("A", 1, 1), ("C", 1, 1), ("T", 2, 1), ("A", 2, 0),
        ("C", 2, 2), ("Y", 2, 0), ("M", 1, 0), ("C", 2, 1), ("T", 3, 0), ("M", 1, 1),
        ("C", 3, 0), ("Y", 2, 1), ("M", 2, 0), ("C", 2, 3), ("T", 3, 1), ("A", 3, 0),
        ("C", 3, 2), ("Y", 3, 0), ("M", 2, 3), ("C", 3, 1), ("Y", 1, 1), ("S", 2, 1),
        ("A", 2, 3), ("C", 1, 3), ("Y", 3, 1), ("S", 3, 1), ("M", 3, 0), ("C", 3, 3),
        ("S", 2, 2), ("M", 1, 2), ("S", 3, 2), ("A", 3, 1), ("S", 3, 3), ("A", 2, 1),
        ("S", 1, 3), ("A", 3, 2), ("S", 0, 1), ("A", 3, 3), ("S", 0, 0), ("A", 2, 2),
        ("S", 0, 2), ("A", 1, 2), ("A", 0, 1), ("S", 0, 3), ("A", 0, 0), ("A", 1, 3),
        ("A", 0, 2), ("A", 0, 3),
    ],
    [
        ("C", 1, 2), ("T", 0, 0), ("T", 2, 0), ("C", 0, 0), ("Y", 1, 0), ("C", 2, 0),
        ("T", 0, 1), ("T", 2, 1), ("C", 1, 1), ("C", 0, 2), ("C", 2, 2), ("Y", 1, 1),
        ("T", 3, 0), ("C", 1, 3), ("C", 3, 0), ("Y", 0, 0), ("Y", 0, 1), ("C", 0, 1),
        ("T", 3, 1), ("R", 0, 0), ("C", 0, 3), ("C", 3, 2), ("Y", 2, 0), ("C", 2, 1),
        ("A", 2, 0), ("M", 2, 1), ("Y", 2, 1), ("C", 2, 3), ("M", 0, 3), ("M", 2, 2),
        ("Y", 3, 0), ("M", 2, 0), ("C", 3, 1), ("S", 1, 1), ("A", 3, 0), ("M", 3, 1),
        ("S", 1, 3), ("Y", 3, 1), ("C", 3, 3), ("S", 2, 3), ("A", 0, 0), ("M", 3, 2),
        ("S", 3, 3), ("M", 0, 1), ("M", 3, 0), ("S", 1, 0), ("A", 2, 3), ("S", 0, 2),
        ("M", 0, 0), ("A", 3, 1), ("S", 1, 2), ("A", 1, 0), ("A", 2, 1), ("A", 0, 1),
        ("A", 3, 2), ("A", 1, 1), ("A", 3, 3), ("A", 0, 2), ("A", 2, 2), ("A", 0, 3),
        ("A", 1, 2), ("A", 1, 3),
    ],
]
CODES = "TYRCSMA"


def encode_plan():
    n = len(PLAN)
    moved = [{(p, q) for what, p, q in steps if what == "M"} for steps in PLAN]
    table = []
    for here, steps in enumerate(PLAN):
        met, row = set(), []
        for what, p, q in steps:
            first = one = two = 0
            if what in "SMA":
                key = (what == "A", p, q // 2)
                first = int(key not in met)
                met.add(key)
            if what == "A":
                one = int((p, q) not in moved[here])
            elif what in "SM":
                one = int(here == 1 and p >= 1 and (p, q) in moved[0])
                if here == 1:
                    two = int(p <= 1 and (3 - p, q) in moved[1])
                else:
                    two = int(p == 0 and (p, q) in moved[1])
            code = CODES.index(what)
            row.append((((((code * 4 + p) * 4 + q) * 2 + first) * 2) + one) * 2 + two)
        table.append(row)
    assert n == 2 and len(table[0]) == len(table[1])
    return table


def fetch(table, first_row, k):
    word = 0
    for w in range(0, len(table[0]), 3):
        pair = [sum(v * 1024**i for i, v in enumerate(row[w : w + 3])) for row in table]
        word = jnp.where(k // 3 == w // 3, jnp.where(first_row, pair[0], pair[1]), word)
    third = k % 3
    word = jnp.where(third == 0, word, jnp.where(third == 1, word // 1024, word // 1024**2))
    return word % 1024


def layer_kernel(
    n_sub,
    q_hbm,
    k_hbm,
    v_hbm,
    residual_hbm,
    proj_hbm,
    gain_hbm,
    ids_hbm,
    gates_hbm,
    wg_hbm,
    wu_hbm,
    wd_hbm,
    o_hbm,
    gain_ref,
    ids_ref,
    gates_ref,
    o_ref,
    o_sem,
    q_all,
    k_all,
    v_all,
    proj,
    residual,
    partial,
    core_far,
    core_near,
    across_near,
    wide_ref,
    q_send,
    q_recv,
    kv_send,
    kv_recv,
    part_send,
    part_recv,
    coef,
    coef_send,
    coef_recv,
    coef_up,
    coef_down,
    coef_z,
    rows,
    outs,
    from_core,
    from_y,
    from_line,
    from_moved,
    wg,
    wu,
    wd,
    load_sem,
    row_recv,
    up_send,
    down_send,
    y_send,
    core_send,
    relay_send,
    core_recv,
    result_send,
    y_recv,
    result_y_send,
    line_recv,
    line_send,
    moved_recv,
    moved_send,
    mate_send,
):
    seq = lax.axis_index("seq")
    z = lax.axis_index("sub")
    y = seq // 2
    c = seq % 2
    tokens = residual.shape[0]
    share = q_all.shape[1]
    heads = share // HD
    length = q_all.shape[0]
    group = QH // KVH
    half = tokens // 2
    me = seq * n_sub + z
    tile = coef.shape[0] // (4 * n_sub)
    quarter = tokens // 4
    plan = encode_plan()
    high = {"sub": z + 1}
    low = {"sub": z - 1}
    across = {"seq": (1 - y) * 2 + c}
    partner = {"seq": y * 2 + 1 - c}
    diagonal = {"seq": (1 - y) * 2 + 1 - c}
    mate = z + 1 - 2 * (z % 2)
    beside = {"sub": mate}
    has_high = z < n_sub - 1
    has_low = z > 0
    corner = jnp.logical_not(jnp.logical_and(has_low, has_high))
    mirrored = jnp.where(z >= n_sub // 2, 1, 0)

    def slot(yy, p, cc):
        return (yy * n_sub + p) * 2 + cc

    def piece_start(index, h):
        return ((index // 2 * 2 + h) * 2 + index % 2) * half

    def piece(ref, index, h):
        return ref.at[pl.ds(pl.multiple_of(piece_start(index, h), half), half), :]

    def remote(src, dst, send, recv, target):
        return pltpu.make_async_remote_copy(
            src_ref=src,
            dst_ref=dst,
            send_sem=send,
            recv_sem=recv,
            device_id=target,
            device_id_type=pl.DeviceIdType.MESH,
        )

    def guarded(condition, action):
        if condition is None:
            action()
        else:
            pl.when(condition)(action)

    def query_part(s, h):
        return q_hbm.at[pl.ds(h * half, half), pl.ds(pl.multiple_of(s * share, share), share)]

    def cache_part(ref, s):
        return ref.at[:, pl.ds(pl.multiple_of(s * heads // group * HD, HD), HD)]

    def token_rows(ref, s):
        return ref.at[pl.ds(pl.multiple_of(s * tokens, tokens), tokens), :]

    def half_rows(s, h):
        return pl.ds(pl.multiple_of(((s // 2 * 2 + h) * 2 + s % 2) * half, half), half)

    barrier = pltpu.get_barrier_semaphore()
    for peer in (across, partner, diagonal):
        pl.semaphore_signal(barrier, 1, device_id=peer, device_id_type=pl.DeviceIdType.MESH)

    @pl.when(has_high)
    def _():
        pl.semaphore_signal(barrier, 1, device_id=high, device_id_type=pl.DeviceIdType.MESH)

    @pl.when(has_low)
    def _():
        pl.semaphore_signal(barrier, 1, device_id=low, device_id_type=pl.DeviceIdType.MESH)

    small = [
        pltpu.make_async_copy(ids_hbm, ids_ref, load_sem.at[8]),
        pltpu.make_async_copy(gates_hbm, gates_ref, load_sem.at[9]),
    ]
    own_parts = [
        pltpu.make_async_copy(cache_part(k_hbm, seq), token_rows(k_all, seq), load_sem.at[1]),
        pltpu.make_async_copy(cache_part(v_hbm, seq), token_rows(v_all, seq), load_sem.at[2]),
        pltpu.make_async_copy(query_part(seq, 0), q_all.at[half_rows(seq, 0), :], load_sem.at[0]),
        pltpu.make_async_copy(query_part(seq, 1), q_all.at[half_rows(seq, 1), :], load_sem.at[11]),
        pltpu.make_async_copy(proj_hbm, proj, load_sem.at[3]),
    ]
    loads = [
        pltpu.make_async_copy(residual_hbm, residual, load_sem.at[7]),
        pltpu.make_async_copy(gain_hbm, gain_ref, load_sem.at[10]),
        pltpu.make_async_copy(wg_hbm, wg, load_sem.at[4]),
        pltpu.make_async_copy(wu_hbm, wu, load_sem.at[5]),
        pltpu.make_async_copy(wd_hbm, wd, load_sem.at[6]),
    ]
    for load in small + own_parts + loads:
        load.start()

    def coef_tile(p, s, count=1):
        return pl.ds(pl.multiple_of((p * 4 + s) * tile, tile), count * tile)

    for load in small:
        load.wait()
    expert = lax.broadcasted_iota(jnp.int32, (tile, tokens), 0)
    ids = ids_ref[...]
    gates = gates_ref[...].astype(jnp.float32)
    weights_here = jnp.zeros((tile, tokens), jnp.float32)
    for k in range(ids.shape[0]):
        weights_here = weights_here + jnp.where(ids[k : k + 1, :] == expert, gates[k : k + 1, :], 0.0)
    coef[coef_tile(z, seq), :] = weights_here.astype(jnp.bfloat16)
    peers = 3 + jnp.where(has_high, 1, 0) + jnp.where(has_low, 1, 0)
    with jax.named_scope("BAR"):
        pl.semaphore_wait(barrier, peers)

    others = (
        ((1 - y) * 2 + c, across),
        ((1 - y) * 2 + 1 - c, diagonal),
        (y * 2 + 1 - c, partner),
    )

    def cache_copies(s, target):
        return (
            remote(
                cache_part(k_hbm, s),
                token_rows(k_all, seq),
                kv_send.at[s],
                kv_recv.at[seq],
                target,
            ),
            remote(
                cache_part(v_hbm, s),
                token_rows(v_all, seq),
                kv_send.at[4 + s],
                kv_recv.at[4 + seq],
                target,
            ),
        )

    def query_copy(s, h, target):
        return remote(
            query_part(s, h),
            q_all.at[half_rows(seq, h), :],
            q_send.at[s * 2 + h],
            q_recv.at[seq * 2 + h],
            target,
        )

    def coef_near(s, target):
        here = coef.at[coef_tile(z, seq), :]
        return remote(here, here, coef_send.at[s], coef_recv.at[seq], target)

    for s, target in others:
        coef_near(s, target).start()
        for copy in cache_copies(s, target):
            copy.start()
    for h in range(2):
        for s, target in others:
            query_copy(s, h, target).start()

    def arrival(ref, s, sem):
        return remote(token_rows(ref, s), token_rows(ref, s), q_send.at[s], sem, partner)

    def coef_hop(p, send, target):
        here = coef.at[coef_tile(p, 0, 4), :]
        return remote(here, here, send.at[p], coef_z.at[p], target)

    def coef_take(p, way):
        coef_hop(p, coef_up, high).wait_recv()

        @pl.when(has_high if way > 0 else has_low)
        def _():
            (coef_hop(p, coef_up, high) if way > 0 else coef_hop(p, coef_down, low)).start()

    def coef_step(d):
        pl.when(z - d >= 0)(lambda: coef_take(z - d, 1))
        pl.when(z + d < n_sub)(lambda: coef_take(z + d, -1))

    for load in own_parts:
        load.wait()
    with jax.named_scope("ARR"):
        for s, _ in others:
            arrival(k_all, s, kv_recv.at[s]).wait_recv()
            arrival(v_all, s, kv_recv.at[4 + s]).wait_recv()

    def half_copy(src_rows, dst, h, at, target):
        return remote(
            partial.at[src_rows, :],
            dst.at[pl.ds(pl.multiple_of(h * half, half), half), :],
            part_send.at[at * 2 + h],
            part_recv.at[at * 2 + h],
            target,
        )

    def far_copy(h):
        return half_copy(half_rows((1 - y) * 2 + 1 - c, h), core_far, h, 0, partner)

    def across_copy(h):
        return half_copy(half_rows((1 - y) * 2 + c, h), across_near, h, 1, across)

    def near_copy(h):
        return half_copy(half_rows(y * 2 + 1 - c, h), core_near, h, 2, partner)

    def half_at(h):
        return pl.ds(pl.multiple_of(h * half, half), half)

    def attend_step(t, carry):
        h = t // 2
        other = jnp.logical_or(t == 1, t == 2)
        yy = jnp.where(other, 1 - y, y)
        at = pl.ds(pl.multiple_of((yy * 2 + h) * tokens, tokens), tokens)

        for cc in range(2):

            @pl.when(yy * 2 + cc != seq)
            def _():
                block = q_all.at[half_rows(yy * 2 + cc, h), :]
                arrived = q_recv.at[(yy * 2 + cc) * 2 + h]
                remote(block, block, q_send.at[0], arrived, partner).wait_recv()

        @pl.when(t == 2)
        def _():
            send_sum(0)

        with jax.named_scope("A1"):
            row = lax.broadcasted_iota(jnp.int32, (tokens, 1), 0)
            row_pos = yy * 2 * tokens + h * half + row + jnp.where(row >= half, tokens - half, 0)
            col_pos = lax.broadcasted_iota(jnp.int32, (tokens, length), 1)
            allowed = row_pos >= col_pos
            scores = lax.dot_general(
                jnp.concatenate([q_all[at, head * HD : (head + 1) * HD] for head in range(heads)], axis=0),
                k_all[...],
                (((1,), (1,)), ((), ())),
                preferred_element_type=jnp.float32,
            )
            chances, totals = [], []
            for head in range(heads):
                raw = jnp.where(allowed, scores[head * tokens : (head + 1) * tokens], -1e30)
                peak = jnp.max(raw, axis=1, keepdims=True)
                weights = jnp.exp2((raw - peak) * (math.log2(math.e) / HD**0.5))
                totals.append(jnp.sum(weights, axis=1, keepdims=True))
                chances.append(weights.astype(jnp.bfloat16))
            mixed = jnp.dot(
                jnp.concatenate(chances, axis=0), v_all[...], preferred_element_type=jnp.float32
            )
            outputs = [
                (mixed[head * tokens : (head + 1) * tokens] * (1.0 / totals[head])).astype(jnp.bfloat16)
                for head in range(heads)
            ]
        partial[at, :] = jnp.dot(
            jnp.concatenate(outputs, axis=1), proj[...], preferred_element_type=jnp.float32
        ).astype(jnp.bfloat16)

        pl.when(other)(lambda: far_copy(h).start())
        pl.when(jnp.logical_not(other))(lambda: near_copy(h).start())

        @pl.when(t == 0)
        def _():
            for s, target in others:
                there = coef.at[coef_tile(z, s), :]
                remote(there, there, coef_send.at[s], coef_recv.at[s], target).wait_recv()
            pl.when(has_high)(lambda: coef_hop(z, coef_up, high).start())
            pl.when(has_low)(lambda: coef_hop(z, coef_down, low).start())

        pl.when(t == 1)(lambda: coef_step(1))
        return carry

    def send_sum(h):
        far_copy(h).wait_recv()
        at = half_rows((1 - y) * 2 + c, h)
        total = partial[at, :].astype(jnp.float32) + core_far[half_at(h), :].astype(jnp.float32)
        partial[at, :] = total.astype(jnp.bfloat16)
        across_copy(h).start()

    with jax.named_scope("ATT"):
        lax.fori_loop(0, 4, attend_step, 0)
    send_sum(1)
    coef_step(2)
    for load in loads[:2]:
        load.wait()

    def finish(h):
        near_copy(h).wait_recv()
        with jax.named_scope("ACR"):
            across_copy(h).wait_recv()
        at = half_at(h)
        hidden = (
            residual[at, :].astype(jnp.float32)
            + partial[half_rows(seq, h), :].astype(jnp.float32)
            + core_near[at, :].astype(jnp.float32)
            + across_near[at, :].astype(jnp.float32)
        ).astype(jnp.bfloat16)
        wide_ref[at, :] = hidden
        wide = hidden.astype(jnp.float32)
        normed = (
            wide
            * lax.rsqrt(jnp.mean(wide * wide, axis=1, keepdims=True) + 1e-06)
            * gain_ref[...].astype(jnp.float32)[None, :]
        ).astype(jnp.bfloat16)
        index = slot(y, z, c)
        rows[pl.ds(pl.multiple_of(piece_start(index, h), half), half), :] = normed
        spread(z, h)

    def row_copy(index, h, send, target):
        here = piece(rows, index, h)
        return remote(here, here, send, row_recv.at[index * 2 + h], target)

    def wait_rows(index, h):
        row_copy(index, h, relay_send.at[0], partner).wait_recv()

    def column_copies(p, h):
        index = slot(y, p, c)
        at = p * 2 + h
        return (
            (jnp.logical_and(p <= z, has_high), row_copy(index, h, up_send.at[at], high)),
            (jnp.logical_and(p >= z, has_low), row_copy(index, h, down_send.at[at], low)),
            (
                jnp.logical_or(p != mate, h == 0),
                row_copy(index, h, y_send.at[at], across),
            ),
            (None, row_copy(index, h, core_send.at[at], partner)),
        )

    def spread(p, h):
        for condition, copy in column_copies(p, h):
            guarded(condition, copy.start)

    def relay_copy(p, h):
        return row_copy(slot(1 - y, p, c), h, relay_send.at[p * 2 + h], partner)

    def result_copy(yy, p, h):
        pair = yy * n_sub + p
        dst = from_core.at[pl.ds(pl.multiple_of(pair * tokens + h * half, half), half), :]
        at = pair * 2 + h
        return remote(
            piece(outs, slot(yy, p, 1 - c), h), dst, result_send.at[at], core_recv.at[at], partner
        )

    mine = (
        lax.broadcasted_iota(jnp.int32, (tile, 128), 0) == me
    ).astype(jnp.float32).astype(jnp.bfloat16)

    def compute(yy, p, h):
        wait_rows(slot(yy, p, 1 - c), h)
        with jax.named_scope("C"):
            at = pl.ds(pl.multiple_of(((yy * n_sub + p) * 2 + h) * tokens, tokens), tokens)
            x = rows[at, :]
            gains = []
            for cc in range(2):
                both = lax.dot_general(
                    coef[coef_tile(p, 2 * yy + cc), :],
                    mine,
                    (((0,), (0,)), ((), ())),
                    preferred_element_type=jnp.float32,
                )
                gains.append(jnp.where(h == 0, both[:half], both[half:]))
            coeff = jnp.concatenate(gains, axis=0)[:, :1]
            gate = jnp.dot(x, wg[...], preferred_element_type=jnp.float32)
            up = jnp.dot(x, wu[...], preferred_element_type=jnp.float32)
            inner = (gate / (1.0 + jnp.exp(-gate)) * up).astype(jnp.bfloat16)
            out = jnp.dot(inner, wd[...], preferred_element_type=jnp.float32)
            outs[at, :] = (out * coeff).astype(jnp.bfloat16)
        result_copy(yy, p, h).start()

    def mate_rows():
        return row_copy(slot(1 - y, z, c), 1, mate_send.at[0], beside)

    finish(0)
    for load in loads[2:]:
        load.wait()
    compute(y, z, 0)
    finish(1)
    coef_step(3)

    def part(index, q):
        return pl.ds(pl.multiple_of(index * tokens + q * quarter, quarter), quarter)

    def sums(index, q):
        start = piece_start(index, q // 2) + q % 2 * quarter
        return pl.ds(pl.multiple_of(start, quarter), quarter)

    def y_copy(p, q):
        at = p * 4 + q
        return remote(
            outs.at[sums(slot(1 - y, p, c), q), :],
            from_y.at[part(p, q), :],
            result_y_send.at[at],
            y_recv.at[at],
            across,
        )

    def passed(yy, p, q, way, buffer, send, recv):
        at = p * 4 + q
        return remote(
            outs.at[sums(slot(yy, p, c), q), :],
            buffer.at[part(way * n_sub + p, q), :],
            send.at[at],
            recv.at[way * 4 * n_sub + at],
            {"sub": z + 1 - 2 * way},
        )

    def line_copy(p, q, way):
        return passed(y, p, q, way, from_line, line_send, line_recv)

    def moved_copy(p, q, way):
        return passed(1 - y, p, q, way, from_moved, moved_send, moved_recv)

    def add_to(index, q, ref, at, q_at):
        here = sums(index, q)
        total = outs[here, :].astype(jnp.float32) + ref[part(at, q_at), :].astype(jnp.float32)
        outs[here, :] = total.astype(jnp.bfloat16)

    def out_copy(q):
        return pltpu.make_async_copy(o_ref.at[part(0, q), :], o_hbm.at[part(0, q), :], o_sem.at[q])

    def toward(p):
        return jnp.where(p > z, 0, 1)

    def act(k, carry):
        entry = fetch(plan, corner, k)
        what = entry // 128
        place = entry // 32 % 4
        q = entry // 8 % 4
        first = entry // 4 % 2
        one = entry // 2 % 2
        two = entry % 2
        p = jnp.where(mirrored == 1, n_sub - 1 - place, place)

        @pl.when(what == CODES.index("T"))
        def _():
            wait_rows(slot(y, p, c), q)
            spread(p, q)

        @pl.when(what == CODES.index("Y"))
        def _():
            wait_rows(slot(1 - y, p, c), q)
            relay_copy(p, q).start()

        @pl.when(what == CODES.index("R"))
        def _():
            mate_rows().start()

        @pl.when(what == CODES.index("C"))
        def _():
            compute(jnp.where(q % 2 == 1, 1 - y, y), p, q // 2)

        @pl.when(jnp.logical_or(what == CODES.index("S"), what == CODES.index("M")))
        def _():
            index = slot(1 - y, p, c)
            pl.when(first == 1)(lambda: result_copy(1 - y, p, q // 2).wait_recv())
            add_to(index, q, from_core, (1 - y) * n_sub + p, q)

            @pl.when(one == 1)
            def _():
                moved_copy(p, q, mirrored).wait_recv()
                add_to(index, q, from_moved, mirrored * n_sub + p, q)

            @pl.when(two == 1)
            def _():
                moved_copy(p, q, 1 - mirrored).wait_recv()
                add_to(index, q, from_moved, (1 - mirrored) * n_sub + p, q)

            pl.when(what == CODES.index("S"))(lambda: y_copy(p, q).start())
            pl.when(what == CODES.index("M"))(lambda: moved_copy(p, q, toward(p)).start())

        @pl.when(what == CODES.index("A"))
        def _():
            index = slot(y, p, c)
            pl.when(first == 1)(lambda: result_copy(y, p, q // 2).wait_recv())
            add_to(index, q, from_core, y * n_sub + p, q)

            @pl.when(one == 1)
            def _():
                y_copy(p, q).wait_recv()
                add_to(index, q, from_y, p, q)

            for way, comes in ((0, p >= z), (1, p <= z)):

                @pl.when(jnp.logical_and(comes, has_low if way == 0 else has_high))
                def _():
                    line_copy(p, q, way).wait_recv()
                    add_to(index, q, from_line, way * n_sub + p, q)

            pl.when(p != z)(lambda: line_copy(p, q, toward(p)).start())

            @pl.when(p == z)
            def _():
                at = part(0, q)
                o_ref[at, :] = (
                    wide_ref[at, :].astype(jnp.float32) + outs[sums(index, q), :].astype(jnp.float32)
                ).astype(jnp.bfloat16)
                out_copy(q).start()

        return carry

    with jax.named_scope("PLAN"):
        lax.fori_loop(0, len(plan[0]), act, 0)

    def drain(k, carry):
        p = k // 2
        h = k % 2
        for condition, copy in column_copies(p, h):
            guarded(condition, copy.wait_send)

        relay_copy(p, h).wait_send()
        result_copy(0, p, h).wait_send()
        result_copy(1, p, h).wait_send()

        @pl.when(h == 0)
        def _():
            pl.when(jnp.logical_and(p <= z, has_high))(lambda: coef_hop(p, coef_up, high).wait_send())
            pl.when(jnp.logical_and(p >= z, has_low))(lambda: coef_hop(p, coef_down, low).wait_send())

        return carry

    lax.fori_loop(0, 2 * n_sub, drain, 0)
    for here, steps in enumerate(PLAN):

        @pl.when(corner == (here == 0))
        def _():
            for what, place, q in steps:
                p = jnp.where(mirrored == 1, n_sub - 1 - place, place)
                if what == "S":
                    y_copy(p, q).wait_send()
                elif what == "M":
                    moved_copy(p, q, toward(p)).wait_send()
                elif what == "A" and place != here:
                    line_copy(p, q, toward(p)).wait_send()

    for s, target in others:
        for copy in cache_copies(s, target):
            copy.wait_send()
        coef_near(s, target).wait_send()
        for h in range(2):
            query_copy(s, h, target).wait_send()
    mate_rows().wait_send()
    for h in range(2):
        far_copy(h).wait_send()
        across_copy(h).wait_send()
        near_copy(h).wait_send()
    for q in range(4):
        out_copy(q).wait()


def layer(queries, keys, values, residual, proj, gain, ids, gates, w_gate, w_up, w_down, n_sub):
    tokens, width = residual.shape
    share = proj.shape[0]
    blocks = 4 * n_sub
    tile = 16 * ((blocks + 15) // 16)
    dma = lambda count: pltpu.SemaphoreType.DMA((count,))
    hbm = pl.BlockSpec(memory_space=pl.ANY)
    bf = jnp.bfloat16
    return pl.pallas_call(
        functools.partial(layer_kernel, n_sub),
        in_specs=[hbm] * 11,
        out_specs=hbm,
        out_shape=jax.ShapeDtypeStruct((tokens, width), bf),
        scratch_shapes=[
            pltpu.VMEM(gain.shape, bf),
            pltpu.VMEM(ids.shape, jnp.int32),
            pltpu.VMEM(gates.shape, bf),
            pltpu.VMEM((tokens, width), bf),
            dma(4),
            pltpu.VMEM((4 * tokens, share), bf),
            pltpu.VMEM((4 * tokens, HD), bf),
            pltpu.VMEM((4 * tokens, HD), bf),
            pltpu.VMEM(proj.shape, bf),
            pltpu.VMEM((tokens, width), bf),
            pltpu.VMEM((4 * tokens, width), bf),
            pltpu.VMEM((tokens, width), bf),
            pltpu.VMEM((tokens, width), bf),
            pltpu.VMEM((tokens, width), bf),
            pltpu.VMEM((tokens, width), bf),
            dma(8),
            dma(8),
            dma(8),
            dma(8),
            dma(6),
            dma(6),
            pltpu.VMEM((blocks * tile, tokens), bf),
            dma(4),
            dma(4),
            dma(n_sub),
            dma(n_sub),
            dma(n_sub),
            pltpu.VMEM((blocks * tokens, width), bf),
            pltpu.VMEM((blocks * tokens, width), bf),
            pltpu.VMEM((2 * n_sub * tokens, width), bf),
            pltpu.VMEM((n_sub * tokens, width), bf),
            pltpu.VMEM((2 * n_sub * tokens, width), bf),
            pltpu.VMEM((2 * n_sub * tokens, width), bf),
            pltpu.VMEM(w_gate.shape, bf),
            pltpu.VMEM(w_up.shape, bf),
            pltpu.VMEM(w_down.shape, bf),
            dma(12),
            dma(2 * blocks),
            dma(2 * n_sub),
            dma(2 * n_sub),
            dma(2 * n_sub),
            dma(2 * n_sub),
            dma(2 * n_sub),
            dma(4 * n_sub),
            dma(4 * n_sub),
            dma(4 * n_sub),
            dma(4 * n_sub),
            dma(8 * n_sub),
            dma(4 * n_sub),
            dma(8 * n_sub),
            dma(4 * n_sub),
            dma(1),
        ],
        compiler_params=pltpu.CompilerParams(
            collective_id=0, has_side_effects=True, vmem_limit_bytes=60 * 2**20
        ),
        name="layer",
    )(queries, keys, values, residual, proj, gain, ids, gates, w_gate, w_up, w_down)


def per_device_dense(
    query_rows,
    key_rows,
    value_rows,
    residual_in,
    out_proj,
    norm_gain,
    expert_ids,
    gate_weights,
    expert_gate,
    expert_up,
    expert_down,
):
    return layer(
        query_rows[0],
        key_rows[0],
        value_rows[0],
        residual_in[0],
        out_proj,
        norm_gain,
        expert_ids[0].T,
        gate_weights[0].T,
        expert_gate[0],
        expert_up[0],
        expert_down[0],
        lax.axis_size("sub"),
    )[None]


def per_device(*args):
    tokens = args[0].shape[1]
    topk = args[6].shape[2]
    n_seq = lax.axis_size("seq")
    experts = n_seq * lax.axis_size("sub")
    cap = max(2, (5 * tokens * topk + 4 * experts - 1) // (4 * experts))
    if 2 * cap >= tokens and n_seq == 4 and lax.axis_size("sub") == 4 and tokens == 128:
        return per_device_dense(*args)
    return per_device_routed(*args)


def solution(mesh):
    placed = (
        P(("grp", "sub"), "seq", None),
        P(("grp", "sub"), "seq", None),
        P(("grp", "sub"), "seq", None),
        P(("grp", "sub"), "seq", None),
        P("seq", None),
        P(),
        P(("grp", "sub"), "seq", None),
        P(("grp", "sub"), "seq", None),
        P(("seq", "sub"), None, None),
        P(("seq", "sub"), None, None),
        P(("seq", "sub"), None, None),
    )
    return jax.shard_map(
        per_device,
        mesh=mesh,
        in_specs=placed,
        out_specs=P(("grp", "sub"), "seq", None),
        check_vma=False,
    )
```
